256 devices in a mesh: frame: 4 (over x), space: 64 (over z, y, core).
Axes of the slice: x: 4, y: 4, z: 8, core: 2. Of those that a mesh axis runs over, the one named last changes fastest.
Arguments:
- queries: bfloat16 [32768, 3072], P(('frame', 'space')), as said below
- keys: bfloat16 [32768, 3072], P(('frame', 'space')), as said below
- values: bfloat16 [32768, 3072], P(('frame', 'space')), may hold values from -5 to 5
- level_weight: float32 [3, 24, 32768], P(None, None, ('frame', 'space')), may hold values from 0.2 to 2
- frame_len: int32 [256, 4], P(('frame', 'space')), may hold values from 1 to 53, 128 in all within a row
- window_back: int32 [256, 4], P(('frame', 'space')), may hold values from 2 to 63
Outputs:
- mixed: bfloat16 [32768, 3072], P(('frame', 'space'))
The draws below stay inside these ranges and needn't reach their ends.
Inputs may be any that keep to these rules, and one draw needn't show every extreme that they name: `queries`: entries up to 60 in magnitude. `keys`: entries up to 4 in magnitude. `frame_len`: each row is the frame lengths of one device's 128 tokens, summing to 128; the longest frame of each row has exactly 53 tokens.
All inputs are finite; a program needn't handle non-finite values.
Results may differ from the reference program's by a relative error of at most 0.0085.
Values may be sent and summed in bfloat16 or wider, within the bound.
A program may use at most 64 MiB of HBM per device.

```python
import math
import jax
import jax.numpy as jnp
import numpy as np
from jax import lax

HEADS = 24
HEAD_DIM = 128
TOK_DEV = 128
FRAMES = 4
LEV = 3
MAXF = 53
SHARDS = 256
TOKENS = 32768
N_FRAME = 4
N_SPACE = 64


def query_key_pair(key):
    base = jax.random.fold_in(key, 7301)
    query_key, key_key = jax.random.split(base, 2)
    shape = (TOKENS, HEADS * HEAD_DIM)
    queries = jnp.clip(jax.random.normal(query_key, shape, jnp.float32), -4.0, 4.0)
    keys = jnp.clip(jax.random.normal(key_key, shape, jnp.float32), -4.0, 4.0)
    return (queries, keys)


def draw_queries(key, part):
    return query_key_pair(key)[0].astype(jnp.bfloat16)


def draw_keys(key, part):
    return query_key_pair(key)[1].astype(jnp.bfloat16)


def with_ends(drawn, rng, least, largest):
    longest = drawn.shape.index(max(drawn.shape))
    spots = []
    for shift in (0, 1):
        where = [jax.random.randint(jax.random.fold_in(rng, axis), (), 0, length) for axis, length in enumerate(drawn.shape)]
        where[longest] = (where[longest] + shift) % drawn.shape[longest]
        spots.append(tuple(where))
    return drawn.at[spots[0]].set(least).at[spots[1]].set(largest)


def block_levels(own_key, shape, shards, low, top_value):
    gain, own = 1.0, jax.random.fold_in(own_key, 6)
    for dim, shards_of in shards:
        heights = jnp.exp(jax.random.uniform(jax.random.fold_in(own, dim), (shards_of,), jnp.float32, low / len(shards), top_value / len(shards)))
        gain = gain * jnp.repeat(heights, shape[dim] // shards_of).reshape([-1 if axis == dim else 1 for axis in range(len(shape))])
    return gain


def split_up(amount, total, limit, slope):
    loads = [(1 << 20) // math.isqrt(grade ** slope) + 1 for grade in range(2, amount + 1)]
    surplus, counts = total - limit - (amount - 1), [1] * (amount - 1)
    while surplus > 0:
        candidates = [i for i in range(amount - 1) if counts[i] < limit]
        mass, budget = sum([loads[i] for i in candidates]), surplus
        for i in candidates:
            addition = min(limit - counts[i], max(1, budget * loads[i] // mass), surplus)
            counts[i] = counts[i] + addition
            surplus = surplus - addition
    return np.array([limit] + counts)


def uneven_parts(stream_key, count, total, bound, slope):
    if count == 2:
        one = jax.random.randint(stream_key, (), max(1, total - bound), min(bound, total - 1) + 1)
        return jnp.stack([one, total - one])
    tallies = jnp.asarray(split_up(count, total, bound, slope), jnp.int32)
    couples = (count - 1) // 2
    giver, taker = tallies[1:1 + 2 * couples:2], tallies[2:2 + 2 * couples:2]
    margin = jnp.minimum(giver - 1, bound - taker)
    passed = jax.random.randint(jax.random.fold_in(stream_key, 1), (couples,), 0, 1 << 20) % (margin + 1)
    tallies = tallies.at[1:1 + 2 * couples:2].set(giver - passed).at[2:2 + 2 * couples:2].set(taker + passed)
    return tallies[jax.random.permutation(jax.random.fold_in(stream_key, 2), count)]


def bell_draw(key, shape, spread, most, cuts=(), kind=jnp.bfloat16):
    array = spread * jax.random.normal(key, shape, jnp.float32)
    if cuts:
        array = array * block_levels(key, shape, cuts, -0.22, 0.18)
    return jnp.clip(array, -most, most).astype(kind)


def setup_inputs(seed: int = 0) -> dict:
    splits = jax.random.split(jax.random.key(seed), 7)
    return {
        "queries": draw_queries(jax.random.fold_in(splits[6], 71), 0),
        "keys": draw_keys(jax.random.fold_in(splits[6], 71), 0),
        "values": bell_draw(splits[2], (TOKENS, HEADS * HEAD_DIM), 1.0, 5.0, ((0, 256),)),
        "level_weight": jnp.clip(jnp.exp(math.log(2.0) - 2.3025851 * jax.random.uniform(splits[3], (LEV, HEADS, TOKENS), jnp.float32) ** block_levels(splits[3], (LEV, HEADS, TOKENS), ((2, 256),), -0.2, 0.2)), 0.2, 2.0),
        "frame_len": jax.vmap(lambda own: uneven_parts(own, FRAMES, TOK_DEV, MAXF, 0))(jax.random.split(splits[4], SHARDS)).reshape((SHARDS, FRAMES)).astype(jnp.int32),
        "window_back": with_ends(jax.random.randint(splits[5], (SHARDS, FRAMES), 2, TOK_DEV // 2), jax.random.fold_in(splits[5], 1), 2, (TOK_DEV // 2) - 1).astype(jnp.int32),
    }


EPSILON = 1e-06

def unit_rows(matrix):
    return (matrix * lax.rsqrt(lax.optimization_barrier(jnp.mean(matrix * matrix, -1, keepdims=True)) + EPSILON)).astype(jnp.bfloat16)

def visible_mask(lengths, backward, count):
    lengths = lengths.astype(jnp.int32)
    backward = backward.astype(jnp.int32)
    starts = jnp.cumsum(lengths) - lengths
    lowest = jnp.maximum(starts - backward, 0)
    position = jnp.arange(count, dtype=jnp.int32)
    inside = (position[:, None] >= starts[None, :]).astype(jnp.int32)
    frame_of = lax.optimization_barrier(jnp.sum(inside, 1)) - 1
    onehot = frame_of[:, None] == jnp.arange(lengths.shape[0], dtype=jnp.int32)[None, :]
    floor_row = lax.optimization_barrier(jnp.sum(jnp.where(onehot, lowest[None, :], 0), 1))
    return (position[None, :] <= position[:, None]) & (position[None, :] >= floor_row[:, None])

def causal_mix(query_heads, key_heads, value_heads, visible, heads, head_dim):
    pieces = []
    for first_head in range(0, heads, 4):
        query_part = query_heads[:, first_head:first_head + 4].astype(jnp.float32)
        key_part = key_heads[:, first_head:first_head + 4].astype(jnp.float32)
        value_part = value_heads[:, first_head:first_head + 4].astype(jnp.float32)
        scores = jnp.einsum('thd,shd->hts', query_part, key_part) / math.sqrt(head_dim)
        scores = jnp.where(visible[None], scores, -jnp.inf)
        row_max = lax.optimization_barrier(jnp.max(scores, -1, keepdims=True))
        weights = jnp.exp(scores - row_max)
        totals = lax.optimization_barrier(jnp.sum(weights, -1))
        rounded = lax.optimization_barrier(weights.astype(jnp.bfloat16)).astype(jnp.float32)
        mixed_part = jnp.einsum('hts,shd->thd', rounded, value_part)
        pieces.append(mixed_part / jnp.transpose(totals)[:, :, None])
    return jnp.concatenate(pieces, 1)

def reference(queries, keys, values, level_weight, frame_len, window_back):
    block_tokens = TOK_DEV * N_SPACE
    key_blocks = keys.reshape(N_FRAME, block_tokens, HEADS, HEAD_DIM)
    value_blocks = values.reshape(N_FRAME, block_tokens, HEADS, HEAD_DIM)

    def block_state(pair):
        key_block, value_block = pair
        normal_k = unit_rows(key_block.astype(jnp.float32)).astype(jnp.float32)
        return jnp.einsum('thd,the->hde', normal_k, value_block.astype(jnp.float32))
    states = lax.map(block_state, (key_blocks, value_blocks))
    tree_depth = N_FRAME.bit_length() - 1
    per_block = []
    for frame_index in range(N_FRAME):
        per_level = []
        for level_index in range(tree_depth):
            lowest_block = frame_index >> level_index + 1 << level_index + 1
            if frame_index >> level_index & 1:
                per_level.append(lax.optimization_barrier(jnp.sum(states[lowest_block:lowest_block + 2 ** level_index], 0)))
            else:
                per_level.append(jnp.zeros_like(states[0]))
        per_block.append(jnp.stack(per_level))
    level_states = jnp.stack(per_block).astype(jnp.bfloat16)
    shard_ids = jnp.arange(SHARDS, dtype=jnp.int32)
    weights_by_shard = jnp.moveaxis(level_weight.reshape(LEV, HEADS, SHARDS, TOK_DEV), 2, 0)

    def one_shard(inputs):
        query_rows, key_rows, value_rows, weight_rows, lengths, backward, shard = inputs
        visible = visible_mask(lengths, backward, TOK_DEV)
        local_mix = causal_mix(query_rows, key_rows, value_rows, visible, HEADS, HEAD_DIM)
        result = local_mix * jnp.transpose(weight_rows[0])[:, :, None]
        normal_q = unit_rows(query_rows.astype(jnp.float32)).astype(jnp.float32)
        own_levels = lax.dynamic_index_in_dim(level_states, (shard // N_SPACE).astype(jnp.int32), 0, keepdims=False)
        for level_index in range(tree_depth):
            level_read = jnp.einsum('thd,hde->the', normal_q, own_levels[level_index].astype(jnp.float32))
            level_scale = 1.0 / math.sqrt(HEAD_DIM * 2 ** level_index * block_tokens)
            result = result + jnp.transpose(weight_rows[1 + level_index])[:, :, None] * (level_scale * level_read)
        return result.reshape(TOK_DEV, HEADS * HEAD_DIM).astype(jnp.bfloat16)
    outputs = lax.map(one_shard, (queries.reshape(SHARDS, TOK_DEV, HEADS, HEAD_DIM), keys.reshape(SHARDS, TOK_DEV, HEADS, HEAD_DIM), values.reshape(SHARDS, TOK_DEV, HEADS, HEAD_DIM), weights_by_shard, frame_len, window_back, shard_ids))
    return outputs.reshape(TOKENS, HEADS * HEAD_DIM)
```

```python
import functools
import math

import jax
import jax.numpy as jnp
from jax import lax
from jax.experimental import pallas as pl
from jax.experimental.pallas import tpu as pltpu
from jax.sharding import PartitionSpec as P

MESH = pl.DeviceIdType.MESH
HEADS = 24
HALF = 12
D = 128
EPS = 1e-06
NY = 4
NZ = 8
CH = 3
CR = CH * D
HR = CR // 2
PR = CR // NZ
ORDER = (0, 1, 7, 2, 6, 3, 5, 4)
GO_RIGHT = (0, 7, 2, 5)


def kernel(
    block_tokens,
    flen,
    wback,
    lw,
    q_hbm,
    k_hbm,
    v_hbm,
    out_hbm,
    q,
    k,
    v,
    bias,
    wrows,
    wt,
    loc,
    qs,
    part,
    sib_out,
    sib_in,
    y_out,
    y_opp,
    y_in,
    z_out,
    z_in,
    x_out,
    x_in,
    lev,
    out,
    load_sem,
    sib_s,
    sib_r,
    y_s,
    y_r,
    z_s,
    z_r,
    x_s,
    x_r,
    gz_s,
    gz_r,
    gy_s,
    gy_r,
    gr_s,
    gr_r,
    gs_s,
    gs_r,
    out_sem,
):
    f = lax.axis_index("frame")
    s = lax.axis_index("space")
    c = lax.rem(s, 2)
    y = lax.rem(s // 2, NY)
    z = s // (2 * NY)
    right = lax.rem(y + 1, NY)
    left = lax.rem(y + NY - 1, NY)
    opp = lax.rem(y + 2, NY)

    def at(zz, yy, cc):
        return (zz * NY + yy) * 2 + cc

    sib = (f, at(z, y, 1 - c))
    to_right = (f, at(z, right, c))
    to_left = (f, at(z, left, c))

    def z_peer(step):
        return (f, at(lax.rem(z + step, NZ), y, c))

    def cols(head, count=1):
        return pl.ds(pl.multiple_of(head * D, D), count * D)

    def send(src, dst, ssem, rsem, dev):
        return pltpu.make_async_remote_copy(
            src_ref=src, dst_ref=dst, send_sem=ssem, recv_sem=rsem, device_id=dev, device_id_type=MESH
        )

    other = cols((1 - c) * HALF, HALF)
    mine = cols(c * HALF, HALF)
    loads = []
    for i, (src, dst, cc) in enumerate(
        ((k_hbm, k, other), (v_hbm, v, other), (k_hbm, k, mine), (v_hbm, v, mine))
    ):
        cp = pltpu.make_async_copy(src.at[:, cc], dst.at[:, cc], load_sem.at[i])
        cp.start()
        loads.append(cp)
    q_load = pltpu.make_async_copy(q_hbm, q, load_sem.at[4])
    q_load.start()

    barrier = pltpu.get_barrier_semaphore()
    peers = [sib, to_right, to_left]
    peers += [z_peer(i) for i in range(1, NZ)]
    peers += [(lax.rem(f + i, 4), s) for i in range(1, 4)]
    for dev in peers:
        pl.semaphore_signal(barrier, inc=1, device_id=dev, device_id_type=MESH)

    row = lax.broadcasted_iota(jnp.int32, (D, D), 0)
    col = lax.broadcasted_iota(jnp.int32, (D, D), 1)
    floor = jnp.full((D, D), 0, jnp.int32)
    start = 0
    for i in range(4):
        low = jnp.maximum(start - wback[0, i], 0)
        floor = jnp.where(row >= start, low, floor)
        start = start + flen[0, i]
    bias[...] = jnp.where((col <= row) & (col >= floor), 0.0, -jnp.inf)
    scale1 = 1.0 / math.sqrt(D * block_tokens)
    scale2 = 1.0 / math.sqrt(D * 2 * block_tokens)
    wrows[...] = jnp.zeros_like(wrows)
    wrows[0:HEADS] = lw[0]
    wrows[HEADS : 2 * HEADS] = jnp.where(f == 2, lw[2] * scale2, lw[1] * scale1)
    wrows[2 * HEADS : 3 * HEADS] = lw[2] * scale2
    wt[...] = jnp.transpose(wrows[...])

    def weight(index):
        return jnp.sum(jnp.where(col == index, wt[...], 0.0), -1, keepdims=True)

    def state(head):
        kk = k[:, cols(head)].astype(jnp.float32)
        kn = (kk * lax.rsqrt(jnp.mean(kk * kk, -1, keepdims=True) + EPS)).astype(jnp.bfloat16)
        return lax.dot_general(
            kn, v[:, cols(head)], (((0,), (0,)), ((), ())), preferred_element_type=jnp.float32
        )

    def attend(first, last):
        @pl.loop(first, last)
        def _(j):
            for i in range(CH):
                h = j * CH + i
                qq = q[:, cols(h)]
                scores = lax.dot_general(
                    qq, k[:, cols(h)], (((1,), (1,)), ((), ())), preferred_element_type=jnp.float32
                )
                scores = scores + bias[...]
                top = jnp.max(scores, -1, keepdims=True)
                p = jnp.exp((scores - top) * (1.0 / math.sqrt(D)))
                total = jnp.sum(p, -1, keepdims=True)
                mix = jnp.dot(p.astype(jnp.bfloat16), v[:, cols(h)], preferred_element_type=jnp.float32)
                loc[:, cols(h)] = mix * (weight(h) / total)
                q32 = qq.astype(jnp.float32)
                r = lax.rsqrt(jnp.mean(q32 * q32, -1, keepdims=True) + EPS)
                qs[0, :, cols(h)] = (q32 * (r * weight(HEADS + h))).astype(jnp.bfloat16)
                qs[1, :, cols(h)] = (q32 * (r * weight(2 * HEADS + h))).astype(jnp.bfloat16)

    def rows(chunk, first=0, count=CR):
        return pl.ds(pl.multiple_of(chunk * CR + first, PR), count)

    def sib_copy(j, yc):
        return send(sib_out.at[rows(yc)], sib_in.at[rows(yc)], sib_s.at[j], sib_r.at[j], sib)

    def chunk_at(j):
        return lax.rem(y + 2 - j + NY, NY)

    loads[0].wait()
    loads[1].wait()

    pl.semaphore_wait(barrier, len(peers))

    y_copies = [
        send(y_out.at[0], y_opp.at[0], y_s.at[0], y_r.at[0], to_right),
        send(y_out.at[1], y_opp.at[1], y_s.at[1], y_r.at[1], to_left),
        send(y_out.at[2], y_in.at[0, pl.ds(HR, HR)], y_s.at[2], y_r.at[2], to_right),
        send(y_out.at[3], y_in.at[1, pl.ds(0, HR)], y_s.at[3], y_r.at[3], to_left),
        send(y_out.at[4], y_in.at[0, pl.ds(0, HR)], y_s.at[4], y_r.at[4], to_right),
        send(y_out.at[5], y_in.at[1, pl.ds(HR, HR)], y_s.at[5], y_r.at[5], to_left),
    ]

    def z_copy(step):
        dst_z = lax.rem(z + step, NZ)
        return send(
            z_out.at[pl.ds(pl.multiple_of(dst_z * PR, PR), PR)],
            z_in.at[step],
            z_s.at[step],
            z_r.at[step],
            z_peer(step),
        )

    def x_copy(src_f, dst_f):
        return send(x_out, x_in.at[src_f], x_s.at[dst_f], x_r.at[src_f], (dst_f, s))

    sending = f < 3

    @pl.when(sending)
    def _():
        @pl.loop(0, NY)
        def _(j):
            yc = chunk_at(j)
            for i in range(CH):
                sib_out[pl.ds(pl.multiple_of(yc * CR + i * D, D), D)] = state(
                    (1 - c) * HALF + yc * CH + i
                ).astype(jnp.bfloat16)
            sib_copy(j, yc).start()

    loads[2].wait()
    loads[3].wait()

    @pl.when(sending)
    def _():
        @pl.loop(0, NY)
        def _(j):
            yc = chunk_at(j)
            for i in range(CH):
                part[pl.ds(pl.multiple_of(yc * CR + i * D, D), D)] = state(c * HALF + yc * CH + i)

        def add_sib(j):
            yc = chunk_at(j)
            sib_copy(j, yc).wait_recv()
            return part[rows(yc)] + sib_in[rows(yc)].astype(jnp.float32)

        total = add_sib(0).astype(jnp.bfloat16)
        y_out[0] = total[:HR]
        y_out[1] = total[HR:]
        y_copies[0].start()
        y_copies[1].start()
        total = add_sib(1)
        part[rows(right)] = total
        y_out[2] = total[HR:].astype(jnp.bfloat16)
        y_copies[2].start()
        total = add_sib(3)
        part[rows(left)] = total
        y_out[3] = total[:HR].astype(jnp.bfloat16)
        y_copies[3].start()
        part[rows(y)] = add_sib(2)

    q_load.wait()
    attend(0, 3)

    @pl.when(sending)
    def _():
        y_copies[0].wait_recv()
        y_out[4] = (part[rows(right, 0, HR)] + y_opp[0].astype(jnp.float32)).astype(jnp.bfloat16)
        y_copies[4].start()
        y_copies[1].wait_recv()
        y_out[5] = (part[rows(left, HR, HR)] + y_opp[1].astype(jnp.float32)).astype(jnp.bfloat16)
        y_copies[5].start()

    attend(3, 5)

    @pl.when(sending)
    def _():
        for i in range(2, 6):
            y_copies[i].wait_recv()
        total = part[rows(y)] + y_in[0].astype(jnp.float32) + y_in[1].astype(jnp.float32)
        part[rows(y)] = total
        z_out[...] = total.astype(jnp.bfloat16)
        for i in (4, 3, 5, 2, 6, 1, 7):
            z_copy(i).start()

    attend(5, 7)

    own_rows = pl.ds(pl.multiple_of(z * PR, PR), PR)

    @pl.when(sending)
    def _():
        total = part[pl.ds(pl.multiple_of(y * CR + z * PR, PR), PR)]
        for i in range(1, NZ):
            z_copy(i).wait_recv()
            total = total + z_in[i].astype(jnp.float32)
        x_out[...] = total.astype(jnp.bfloat16)

        for src in range(3):

            @pl.when(f == src)
            def _():
                for dst in range(3, src, -1):
                    x_copy(src, dst).start()

    attend(7, 8)

    chunk = c * NY + y
    piece = pl.ds(pl.multiple_of(chunk * CR + z * PR, PR), PR)

    @pl.when(f == 1)
    def _():
        x_copy(0, 1).wait_recv()
        lev[0, piece] = x_in[0]

    @pl.when(f == 2)
    def _():
        x_copy(0, 2).wait_recv()
        x_copy(1, 2).wait_recv()
        lev[0, piece] = (x_in[0].astype(jnp.float32) + x_in[1].astype(jnp.float32)).astype(jnp.bfloat16)

    @pl.when(f == 3)
    def _():
        for src in range(3):
            x_copy(src, 3).wait_recv()
        lev[0, piece] = x_in[2]
        lev[1, piece] = (x_in[0].astype(jnp.float32) + x_in[1].astype(jnp.float32)).astype(jnp.bfloat16)

    def put(head):
        cp = pltpu.make_async_copy(out.at[:, cols(head, CH)], out_hbm.at[:, cols(head, CH)], out_sem.at[head // CH])
        cp.start()

    def gather(n):
        def block(yc, step):
            zz = lax.rem(z + NZ - step, NZ)
            at_row = pl.multiple_of((c * NY + yc) * CR + zz * PR, PR)
            return lev.at[pl.ds(0, n), pl.ds(at_row, PR)]

        def gz(step):
            return send(block(y, 0), block(y, 0), gz_s.at[step], gz_r.at[step], z_peer(step))

        def gy(side, step):
            dev = to_right if side == 0 else to_left
            return send(block(y, step), block(y, step), gy_s.at[side, step], gy_r.at[side, step], dev)

        def relay(step):
            if step in GO_RIGHT:
                return send(block(left, step), block(left, step), gr_s.at[step], gr_r.at[step], to_right)
            return send(block(right, step), block(right, step), gr_s.at[step], gr_r.at[step], to_left)

        def whole(yc, cc):
            return lev.at[pl.ds(0, n), pl.ds(pl.multiple_of((cc * NY + yc) * CR, CR), CR)]

        def share(j, yc):
            return send(whole(yc, c), whole(yc, c), gs_s.at[j], gs_r.at[j], sib)

        def share_piece(step):
            return send(block(opp, step), block(opp, step), gs_s.at[3 + step], gs_r.at[3 + step], sib)

        def read(chunk_index):
            for i in range(CH):
                h = chunk_index * CH + i
                value = loc[:, cols(h)]
                for m in range(n):
                    value = value + jnp.dot(
                        qs[m, :, cols(h)], lev[m, pl.ds(pl.multiple_of(h * D, D), D)], preferred_element_type=jnp.float32
                    )
                out[:, cols(h)] = value.astype(jnp.bfloat16)
            put(chunk_index * CH)

        for step in (4, 3, 5, 2, 6, 1, 7):
            gz(step).start()
        for i in range(NZ + 2):
            if i < NZ:
                step = ORDER[i]
                if step:
                    gz(step).wait_recv()
                gy(0, step).start()
                gy(1, step).start()
                if i == NZ - 1:
                    share(0, y).start()
            if 1 <= i <= NZ:
                step = ORDER[i - 1]
                gy(0, step).wait_recv()
                gy(1, step).wait_recv()
                relay(step).start()
                if i == NZ:
                    share(1, left).start()
                    share(2, right).start()
            if i >= 2:
                step = ORDER[i - 2]
                relay(step).wait_recv()
                share_piece(step).start()
        read(c * NY + y)
        read(c * NY + left)
        read(c * NY + right)
        for j, yc in enumerate((y, left, right)):
            share(j, yc).wait_recv()
            read((1 - c) * NY + yc)
        read(c * NY + opp)
        for step in ORDER:
            share_piece(step).wait_recv()
        read((1 - c) * NY + opp)
        for step in range(NZ):
            if step:
                gz(step).wait_send()
            gy(0, step).wait_send()
            gy(1, step).wait_send()
            relay(step).wait_send()
            share_piece(step).wait_send()
        for j, yc in enumerate((y, left, right)):
            share(j, yc).wait_send()

    @pl.when(f == 0)
    def _():
        @pl.loop(0, 2 * NY)
        def _(j):
            out[:, cols(j * CH, CH)] = loc[:, cols(j * CH, CH)].astype(jnp.bfloat16)
            put(j * CH)

    @pl.when((f == 1) | (f == 2))
    def _():
        gather(1)

    @pl.when(f == 3)
    def _():
        gather(2)

    @pl.when(sending)
    def _():
        for j in range(NY):
            sib_copy(j, chunk_at(j)).wait_send()
        for cp in y_copies:
            cp.wait_send()
        for i in range(1, NZ):
            z_copy(i).wait_send()
        for src in range(3):

            @pl.when(f == src)
            def _():
                for dst in range(3, src, -1):
                    x_copy(src, dst).wait_send()

    for j in range(2 * NY):
        pltpu.make_async_copy(
            out.at[:, pl.ds(j * CR, CR)], out_hbm.at[:, pl.ds(j * CR, CR)], out_sem.at[j]
        ).wait()


def body(space_count, queries, keys, values, level_weight, frame_len, window_back):
    tok, width = queries.shape
    f32, bf16 = jnp.float32, jnp.bfloat16
    dma = pltpu.SemaphoreType.DMA
    anyspec = pl.BlockSpec(memory_space=pl.ANY)
    smem = pl.BlockSpec(memory_space=pltpu.SMEM)
    return pl.pallas_call(
        functools.partial(kernel, tok * space_count),
        out_shape=jax.ShapeDtypeStruct((tok, width), bf16),
        in_specs=[smem, smem, pl.BlockSpec(memory_space=pltpu.VMEM), anyspec, anyspec, anyspec],
        out_specs=anyspec,
        scratch_shapes=[
            pltpu.VMEM((tok, width), bf16),
            pltpu.VMEM((tok, width), bf16),
            pltpu.VMEM((tok, width), bf16),
            pltpu.VMEM((D, D), f32),
            pltpu.VMEM((D, D), f32),
            pltpu.VMEM((D, D), f32),
            pltpu.VMEM((tok, width), f32),
            pltpu.VMEM((2, tok, width), bf16),
            pltpu.VMEM((HALF * D, D), f32),
            pltpu.VMEM((HALF * D, D), bf16),
            pltpu.VMEM((HALF * D, D), bf16),
            pltpu.VMEM((6, HR, D), bf16),
            pltpu.VMEM((2, HR, D), bf16),
            pltpu.VMEM((2, CR, D), bf16),
            pltpu.VMEM((CR, D), bf16),
            pltpu.VMEM((NZ, PR, D), bf16),
            pltpu.VMEM((PR, D), bf16),
            pltpu.VMEM((3, PR, D), bf16),
            pltpu.VMEM((2, HEADS * D, D), bf16),
            pltpu.VMEM((tok, width), bf16),
            dma((5,)),
            dma((NY,)),
            dma((NY,)),
            dma((6,)),
            dma((6,)),
            dma((NZ,)),
            dma((NZ,)),
            dma((4,)),
            dma((4,)),
            dma((NZ,)),
            dma((NZ,)),
            dma((2, NZ)),
            dma((2, NZ)),
            dma((NZ,)),
            dma((NZ,)),
            dma((NZ + 3,)),
            dma((NZ + 3,)),
            dma((2 * NY,)),
        ],
        compiler_params=pltpu.CompilerParams(collective_id=0, has_side_effects=True),
    )(frame_len, window_back, level_weight, queries, keys, values)


def solution(mesh):
    return jax.shard_map(
        functools.partial(body, mesh.shape["space"]),
        mesh=mesh,
        in_specs=(
            P(("frame", "space"), None),
            P(("frame", "space"), None),
            P(("frame", "space"), None),
            P(None, None, ("frame", "space")),
            P(("frame", "space"), None),
            P(("frame", "space"), None),
        ),
        out_specs=P(("frame", "space"), None),
        check_vma=False,
    )
```

```python
import contextlib
import functools
import math

import jax
import jax.numpy as jnp
from jax import lax
from jax.experimental import pallas as pl
from jax.experimental.pallas import tpu as pltpu
from jax.sharding import PartitionSpec as P

MESH = pl.DeviceIdType.MESH
HEADS = 24
HALF = 12
D = 128
EPS = 1e-06
NY = 4
NZ = 8
CH = 3
CR = CH * D
HR = CR // 2
PR = CR // NZ
ORDER = (0, 1, 7, 2, 6, 3, 5, 4)
GO_RIGHT = (0, 7, 2, 5)


def scope(name):
    return contextlib.nullcontext()


def kernel(
    block_tokens,
    flen_hbm,
    wback_hbm,
    lw_hbm,
    q_hbm,
    k_hbm,
    v_hbm,
    out,
    flen,
    wback,
    lw,
    q,
    k,
    v,
    bias,
    wrows,
    wt,
    loc,
    qs,
    part,
    sib_out,
    sib_in,
    y_out,
    y_opp,
    y_in,
    z_out,
    z_in,
    x_out,
    x_in,
    lev,
    load_sem,
    misc_sem,
    step_sem,
    sib_s,
    sib_r,
    y_s,
    y_r,
    z_s,
    z_r,
    x_s,
    x_r,
    gz_s,
    gz_r,
    gy_s,
    gy_r,
    gr_s,
    gr_r,
    gs_s,
    gs_r,
):
    f = lax.axis_index("frame")
    s = lax.axis_index("space")
    c = lax.rem(s, 2)
    y = lax.rem(s // 2, NY)
    z = s // (2 * NY)
    right = lax.rem(y + 1, NY)
    left = lax.rem(y + NY - 1, NY)
    opp = lax.rem(y + 2, NY)

    def at(zz, yy, cc):
        return (zz * NY + yy) * 2 + cc

    sib = (f, at(z, y, 1 - c))
    to_right = (f, at(z, right, c))
    to_left = (f, at(z, left, c))

    def z_peer(step):
        return (f, at(lax.rem(z + step, NZ), y, c))

    def cols(head, count=1):
        return pl.ds(pl.multiple_of(head * D, D), count * D)

    def send(src, dst, ssem, rsem, dev):
        return pltpu.make_async_remote_copy(
            src_ref=src, dst_ref=dst, send_sem=ssem, recv_sem=rsem, device_id=dev, device_id_type=MESH
        )

    class Group:
        def __init__(self, copies):
            self.copies = copies

        def start(self):
            for cp in self.copies:
                cp.start()

        def wait_recv(self):
            for cp in self.copies:
                cp.wait_recv()

        def wait_send(self):
            for cp in self.copies:
                cp.wait_send()

    def chunk_at(j):
        return (opp, right, left, y)[j]

    def load(j, half, which):
        src, dst = ((k_hbm, k), (v_hbm, v))[which]
        side = (1 - c, c)[half]
        span = cols(side * HALF + chunk_at(j) * CH, CH)
        return pltpu.make_async_copy(src.at[:, span], dst.at[:, span], load_sem.at[j, half, which])

    for j in range(NY):
        for half in range(2):
            for which in range(2):
                load(j, half, which).start()
    small = [
        pltpu.make_async_copy(src, dst, misc_sem.at[i])
        for i, (src, dst) in enumerate(((flen_hbm, flen), (wback_hbm, wback), (lw_hbm, lw), (q_hbm, q)))
    ]
    for cp in small:
        cp.start()

    barrier = pltpu.get_barrier_semaphore()
    z_next = (z_peer(1), z_peer(NZ - 1))
    x_next = ((lax.rem(f + 1, 4), s), (lax.rem(f + 3, 4), s))

    def signal(sem, devices):
        for dev in devices:
            pl.semaphore_signal(sem, inc=1, device_id=dev, device_id_type=MESH)

    signal(barrier, (sib, to_right, to_left, *z_next, *x_next))

    col = lax.broadcasted_iota(jnp.int32, (D, D), 1)

    def weight(index):
        return jnp.sum(jnp.where(col == index, wt[...], 0.0), -1, keepdims=True)

    def state(head):
        kk = k[:, cols(head)].astype(jnp.float32)
        kn = (kk * lax.rsqrt(jnp.mean(kk * kk, -1, keepdims=True) + EPS)).astype(jnp.bfloat16)
        return lax.dot_general(
            kn, v[:, cols(head)], (((0,), (0,)), ((), ())), preferred_element_type=jnp.float32
        )

    def attend(first, last):
        @pl.loop(first, last)
        def _(j):
            for i in range(CH):
                h = j * CH + i
                qq = q[:, cols(h)]
                scores = lax.dot_general(
                    qq, k[:, cols(h)], (((1,), (1,)), ((), ())), preferred_element_type=jnp.float32
                )
                scores = scores + bias[...]
                top = jnp.max(scores, -1, keepdims=True)
                p = jnp.exp((scores - top) * (1.0 / math.sqrt(D)))
                total = jnp.sum(p, -1, keepdims=True)
                mix = jnp.dot(p.astype(jnp.bfloat16), v[:, cols(h)], preferred_element_type=jnp.float32)
                loc[:, cols(h)] = mix * (weight(h) / total)
                q32 = qq.astype(jnp.float32)
                r = lax.rsqrt(jnp.mean(q32 * q32, -1, keepdims=True) + EPS)
                qs[0, :, cols(h)] = (q32 * (r * weight(HEADS + h))).astype(jnp.bfloat16)
                qs[1, :, cols(h)] = (q32 * (r * weight(2 * HEADS + h))).astype(jnp.bfloat16)

    def rows(chunk, first=0, count=CR):
        return pl.ds(pl.multiple_of(chunk * CR + first, PR), count)

    def sib_copy(j, yc):
        return send(sib_out.at[rows(yc)], sib_in.at[rows(yc)], sib_s.at[j], sib_r.at[j], sib)


    y_copies = [
        send(y_out.at[0], y_opp.at[0], y_s.at[0], y_r.at[0], to_right),
        send(y_out.at[1], y_opp.at[1], y_s.at[1], y_r.at[1], to_left),
        send(y_out.at[2], y_in.at[0, pl.ds(HR, HR)], y_s.at[2], y_r.at[2], to_right),
        send(y_out.at[3], y_in.at[1, pl.ds(0, HR)], y_s.at[3], y_r.at[3], to_left),
        send(y_out.at[4], y_in.at[0, pl.ds(0, HR)], y_s.at[4], y_r.at[4], to_right),
        send(y_out.at[5], y_in.at[1, pl.ds(HR, HR)], y_s.at[5], y_r.at[5], to_left),
    ]

    def z_copy(step):
        dst_z = lax.rem(z + step, NZ)
        return send(
            z_out.at[pl.ds(pl.multiple_of(dst_z * PR, PR), PR)],
            z_in.at[step],
            z_s.at[step],
            z_r.at[step],
            z_peer(step),
        )

    def x_copy(src_f, dst_f):
        return send(x_out, x_in.at[src_f], x_s.at[dst_f], x_r.at[src_f], (dst_f, s))

    sending = f < 3

    def states(j, half):
        with scope("st"):
            load(j, half, 0).wait()
            load(j, half, 1).wait()
            yc = chunk_at(j)
            side = (1 - c, c)[half]
            for i in range(CH):
                value = state(side * HALF + yc * CH + i)
                span = pl.ds(pl.multiple_of(yc * CR + i * D, D), D)
                if half == 0:
                    sib_out[span] = value.astype(jnp.bfloat16)
                else:
                    part[span] = value

    def add_sib(j):
        yc = chunk_at(j)
        with scope("sw"):
            sib_copy(j, yc).wait_recv()
        return part[rows(yc)] + sib_in[rows(yc)].astype(jnp.float32)

    def send_opp():
        total = add_sib(0).astype(jnp.bfloat16)
        y_out[0] = total[:HR]
        y_out[1] = total[HR:]
        y_copies[0].start()
        y_copies[1].start()

    def send_right():
        total = add_sib(1)
        part[rows(right)] = total
        y_out[2] = total[HR:].astype(jnp.bfloat16)
        y_copies[2].start()

    def send_left():
        total = add_sib(2)
        part[rows(left)] = total
        y_out[3] = total[:HR].astype(jnp.bfloat16)
        y_copies[3].start()

    @pl.when(sending)
    def _():
        states(0, 0)

    with scope("barrier"):
        pl.semaphore_wait(barrier, 7)
    signal(step_sem.at[0], z_next)
    signal(step_sem.at[3], x_next)

    @pl.when(sending)
    def _():
        sib_copy(0, chunk_at(0)).start()
        states(0, 1)
        states(1, 0)
        sib_copy(1, chunk_at(1)).start()
        states(1, 1)

    with scope("b1"):
        pl.semaphore_wait(step_sem.at[0], 2)
    signal(step_sem.at[1], z_next)

    @pl.when(sending)
    def _():
        send_opp()
        states(2, 0)
        sib_copy(2, chunk_at(2)).start()
        states(2, 1)
        send_right()
        states(3, 0)
        sib_copy(3, chunk_at(3)).start()
        states(3, 1)
        send_left()

    with scope("b2"):
        pl.semaphore_wait(step_sem.at[1], 2)
    signal(step_sem.at[2], z_next)

    @pl.when(sending)
    def _():
        part[rows(y)] = add_sib(3)

    @pl.when(jnp.logical_not(sending))
    def _():
        for j in range(NY):
            for half in range(2):
                load(j, half, 0).wait()
                load(j, half, 1).wait()

    for cp in small:
        cp.wait()
    row = lax.broadcasted_iota(jnp.int32, (D, D), 0)
    floor = jnp.full((D, D), 0, jnp.int32)
    start = 0
    for i in range(4):
        low = jnp.maximum(start - wback[0, i], 0)
        floor = jnp.where(row >= start, low, floor)
        start = start + flen[0, i]
    bias[...] = jnp.where((col <= row) & (col >= floor), 0.0, -jnp.inf)
    scale1 = 1.0 / math.sqrt(D * block_tokens)
    scale2 = 1.0 / math.sqrt(D * 2 * block_tokens)
    wrows[...] = jnp.zeros_like(wrows)
    wrows[0:HEADS] = lw[0]
    wrows[HEADS : 2 * HEADS] = jnp.where(f == 2, lw[2] * scale2, lw[1] * scale1)
    wrows[2 * HEADS : 3 * HEADS] = lw[2] * scale2
    wt[...] = jnp.transpose(wrows[...])

    with scope("att0"):
        attend(0, 2)

    @pl.when(sending)
    def _():
        with scope("yw"):
            y_copies[0].wait_recv()
        y_out[4] = (part[rows(right, 0, HR)] + y_opp[0].astype(jnp.float32)).astype(jnp.bfloat16)
        y_copies[4].start()
        with scope("yw"):
            y_copies[1].wait_recv()
        y_out[5] = (part[rows(left, HR, HR)] + y_opp[1].astype(jnp.float32)).astype(jnp.bfloat16)
        y_copies[5].start()

    with scope("att1"):
        attend(2, 4)
    with scope("b3"):
        pl.semaphore_wait(step_sem.at[2], 2)
        pl.semaphore_wait(step_sem.at[3], 2)

    @pl.when(sending)
    def _():
        with scope("yw2"):
            for i in range(2, 6):
                y_copies[i].wait_recv()
        total = part[rows(y)] + y_in[0].astype(jnp.float32) + y_in[1].astype(jnp.float32)
        part[rows(y)] = total
        z_out[...] = total.astype(jnp.bfloat16)
        for i in (4, 3, 5, 2, 6, 1, 7):
            z_copy(i).start()

    with scope("att2"):
        attend(4, 8)

    @pl.when(sending)
    def _():
        total = part[pl.ds(pl.multiple_of(y * CR + z * PR, PR), PR)]
        for i in range(1, NZ):
            with scope("zw"):
                z_copy(i).wait_recv()
            total = total + z_in[i].astype(jnp.float32)
        x_out[...] = total.astype(jnp.bfloat16)

        for src in range(3):

            @pl.when(f == src)
            def _():
                for dst in range(3, src, -1):
                    x_copy(src, dst).start()

    chunk = c * NY + y
    piece = pl.ds(pl.multiple_of(chunk * CR + z * PR, PR), PR)

    @pl.when(f == 1)
    def _():
        with scope("xw"):
            x_copy(0, 1).wait_recv()
        lev[0, piece] = x_in[0]

    @pl.when(f == 2)
    def _():
        with scope("xw"):
            x_copy(0, 2).wait_recv()
        with scope("xw"):
            x_copy(1, 2).wait_recv()
        lev[0, piece] = (x_in[0].astype(jnp.float32) + x_in[1].astype(jnp.float32)).astype(jnp.bfloat16)

    @pl.when(f == 3)
    def _():
        for src in range(3):
            with scope("xw"):
                x_copy(src, 3).wait_recv()
        lev[0, piece] = x_in[2]
        lev[1, piece] = (x_in[0].astype(jnp.float32) + x_in[1].astype(jnp.float32)).astype(jnp.bfloat16)

    def gather(n):
        def move(at_row, count, ssem, rsem, dev):
            span = pl.ds(pl.multiple_of(at_row, PR), count)
            return Group(
                [send(lev.at[m, span], lev.at[m, span], ssem.at[m], rsem.at[m], dev) for m in range(n)]
            )

        def at_piece(yc, step):
            return (c * NY + yc) * CR + lax.rem(z + NZ - step, NZ) * PR

        def gz(step):
            return move(at_piece(y, 0), PR, gz_s.at[step], gz_r.at[step], z_peer(step))

        def gy(side, step):
            dev = to_right if side == 0 else to_left
            return move(at_piece(y, step), PR, gy_s.at[side, step], gy_r.at[side, step], dev)

        def relay(step):
            if step in GO_RIGHT:
                return move(at_piece(left, step), PR, gr_s.at[step], gr_r.at[step], to_right)
            return move(at_piece(right, step), PR, gr_s.at[step], gr_r.at[step], to_left)

        def share(j, yc):
            return move((c * NY + yc) * CR, CR, gs_s.at[j], gs_r.at[j], sib)

        def share_piece(step):
            return move(at_piece(opp, step), PR, gs_s.at[3 + step], gs_r.at[3 + step], sib)

        def read(chunk_index):
            for i in range(CH):
                h = chunk_index * CH + i
                value = loc[:, cols(h)]
                for m in range(n):
                    value = value + jnp.dot(
                        qs[m, :, cols(h)], lev[m, pl.ds(pl.multiple_of(h * D, D), D)], preferred_element_type=jnp.float32
                    )
                out[:, cols(h)] = value.astype(jnp.bfloat16)

        for step in (4, 3, 5, 2, 6, 1, 7):
            gz(step).start()
        for step in ORDER:
            if step:
                with scope("gzw%d" % step):
                    gz(step).wait_recv()
            gy(0, step).start()
            gy(1, step).start()
        share(0, y).start()
        read(c * NY + y)
        for step in ORDER:
            with scope("gyw%d" % step):
                gy(0, step).wait_recv()
                gy(1, step).wait_recv()
            relay(step).start()
        share(1, left).start()
        share(2, right).start()
        with scope("sw0"):
            share(0, y).wait_recv()
        read((1 - c) * NY + y)
        read(c * NY + left)
        read(c * NY + right)
        for step in ORDER:
            with scope("grw%d" % step):
                relay(step).wait_recv()
            share_piece(step).start()
        for j, yc in ((1, left), (2, right)):
            with scope("sw%d" % j):
                share(j, yc).wait_recv()
            read((1 - c) * NY + yc)
        read(c * NY + opp)
        for step in ORDER:
            with scope("gsw%d" % step):
                share_piece(step).wait_recv()
        read((1 - c) * NY + opp)
        for step in range(NZ):
            if step:
                gz(step).wait_send()
            gy(0, step).wait_send()
            gy(1, step).wait_send()
            relay(step).wait_send()
            share_piece(step).wait_send()
        for j, yc in enumerate((y, left, right)):
            share(j, yc).wait_send()

    @pl.when(f == 0)
    def _():
        @pl.loop(0, 2 * NY)
        def _(j):
            out[:, cols(j * CH, CH)] = loc[:, cols(j * CH, CH)].astype(jnp.bfloat16)

    @pl.when((f == 1) | (f == 2))
    def _():
        gather(1)

    @pl.when(f == 3)
    def _():
        gather(2)

    @pl.when(sending)
    def _():
        for j in range(NY):
            sib_copy(j, chunk_at(j)).wait_send()
        for cp in y_copies:
            cp.wait_send()
        for i in range(1, NZ):
            z_copy(i).wait_send()
        for src in range(3):

            @pl.when(f == src)
            def _():
                for dst in range(3, src, -1):
                    x_copy(src, dst).wait_send()


def body(space_count, queries, keys, values, level_weight, frame_len, window_back):
    tok, width = queries.shape
    f32, bf16 = jnp.float32, jnp.bfloat16
    dma = pltpu.SemaphoreType.DMA
    anyspec = pl.BlockSpec(memory_space=pl.ANY)
    return pl.pallas_call(
        functools.partial(kernel, tok * space_count),
        out_shape=pltpu.VMEM((tok, width), bf16),
        in_specs=[anyspec] * 6,
        out_specs=pl.BlockSpec(memory_space=pltpu.VMEM),
        scratch_shapes=[
            pltpu.SMEM((1, 4), jnp.int32),
            pltpu.SMEM((1, 4), jnp.int32),
            pltpu.VMEM(level_weight.shape, f32),
            pltpu.VMEM((tok, width), bf16),
            pltpu.VMEM((tok, width), bf16),
            pltpu.VMEM((tok, width), bf16),
            pltpu.VMEM((D, D), f32),
            pltpu.VMEM((D, D), f32),
            pltpu.VMEM((D, D), f32),
            pltpu.VMEM((tok, width), f32),
            pltpu.VMEM((2, tok, width), bf16),
            pltpu.VMEM((HALF * D, D), f32),
            pltpu.VMEM((HALF * D, D), bf16),
            pltpu.VMEM((HALF * D, D), bf16),
            pltpu.VMEM((6, HR, D), bf16),
            pltpu.VMEM((2, HR, D), bf16),
            pltpu.VMEM((2, CR, D), bf16),
            pltpu.VMEM((CR, D), bf16),
            pltpu.VMEM((NZ, PR, D), bf16),
            pltpu.VMEM((PR, D), bf16),
            pltpu.VMEM((3, PR, D), bf16),
            pltpu.VMEM((2, HEADS * D, D), bf16),
            dma((NY, 2, 2)),
            dma((4,)),
            pltpu.SemaphoreType.REGULAR((4,)),
            dma((NY,)),
            dma((NY,)),
            dma((6,)),
            dma((6,)),
            dma((NZ,)),
            dma((NZ,)),
            dma((4,)),
            dma((4,)),
            dma((NZ, 2)),
            dma((NZ, 2)),
            dma((2, NZ, 2)),
            dma((2, NZ, 2)),
            dma((NZ, 2)),
            dma((NZ, 2)),
            dma((NZ + 3, 2)),
            dma((NZ + 3, 2)),
        ],
        compiler_params=pltpu.CompilerParams(collective_id=0, has_side_effects=True),
    )(frame_len, window_back, level_weight, queries, keys, values)


def solution(mesh):
    return jax.shard_map(
        functools.partial(body, mesh.shape["space"]),
        mesh=mesh,
        in_specs=(
            P(("frame", "space"), None),
            P(("frame", "space"), None),
            P(("frame", "space"), None),
            P(None, None, ("frame", "space")),
            P(("frame", "space"), None),
            P(("frame", "space"), None),
        ),
        out_specs=P(("frame", "space"), None),
        check_vma=False,
    )
```

```python
import contextlib
import functools
import math

import jax
import jax.numpy as jnp
from jax import lax
from jax.experimental import pallas as pl
from jax.experimental.pallas import tpu as pltpu
from jax.sharding import PartitionSpec as P

MESH = pl.DeviceIdType.MESH
HEADS = 24
HALF = 12
D = 128
EPS = 1e-06
NY = 4
NZ = 8
CH = 3
CR = CH * D
PR = CR // NZ
ORDER = (0, 1, 7, 2, 6, 3, 5, 4)


def scope(name):
    return contextlib.nullcontext()


def kernel(
    block_tokens,
    flen_hbm,
    wback_hbm,
    lw_hbm,
    q_hbm,
    k_hbm,
    v_hbm,
    out,
    flen,
    wback,
    lw,
    q,
    k,
    v,
    bias,
    wrows,
    wt,
    loc,
    qs,
    part,
    sib_out,
    sib_in,
    y_out,
    y_in,
    z_out,
    z_in,
    x_out,
    x_in,
    lev,
    load_sem,
    misc_sem,
    step_sem,
    sib_s,
    sib_r,
    y_s,
    y_r,
    z_s,
    z_r,
    x_s,
    x_r,
    gz_s,
    gz_r,
    gy_s,
    gy_r,
    gs_s,
    gs_r,
):
    f = lax.axis_index("frame")
    s = lax.axis_index("space")
    c = lax.rem(s, 2)
    y = lax.rem(s // 2, NY)
    z = s // (2 * NY)
    right = lax.rem(y + 1, NY)
    left = lax.rem(y + NY - 1, NY)
    opp = lax.rem(y + 2, NY)

    def at(zz, yy, cc):
        return (zz * NY + yy) * 2 + cc

    sib = (f, at(z, y, 1 - c))
    to_right = (f, at(z, right, c))
    to_left = (f, at(z, left, c))
    to_opp = (f, at(z, opp, c))
    across = ((to_opp, opp), (to_right, right), (to_left, left))

    def z_peer(step):
        return (f, at(lax.rem(z + step, NZ), y, c))

    def cols(head, count=1):
        return pl.ds(pl.multiple_of(head * D, D), count * D)

    def send(src, dst, ssem, rsem, dev):
        return pltpu.make_async_remote_copy(
            src_ref=src, dst_ref=dst, send_sem=ssem, recv_sem=rsem, device_id=dev, device_id_type=MESH
        )

    class Group:
        def __init__(self, copies):
            self.copies = copies

        def start(self):
            for cp in self.copies:
                cp.start()

        def wait_recv(self):
            for cp in self.copies:
                cp.wait_recv()

        def wait_send(self):
            for cp in self.copies:
                cp.wait_send()

    def chunk_at(j):
        return (opp, right, left, y)[j]

    def load(j, half, which):
        src, dst = ((k_hbm, k), (v_hbm, v))[which]
        side = (1 - c, c)[half]
        span = cols(side * HALF + chunk_at(j) * CH, CH)
        return pltpu.make_async_copy(src.at[:, span], dst.at[:, span], load_sem.at[j, half, which])

    for j in range(NY):
        for half in range(2):
            for which in range(2):
                load(j, half, which).start()
    small = [
        pltpu.make_async_copy(src, dst, misc_sem.at[i])
        for i, (src, dst) in enumerate(((flen_hbm, flen), (wback_hbm, wback), (lw_hbm, lw), (q_hbm, q)))
    ]
    for cp in small:
        cp.start()

    barrier = pltpu.get_barrier_semaphore()
    z_next = (z_peer(1), z_peer(NZ - 1))
    x_next = ((lax.rem(f + 1, 4), s), (lax.rem(f + 3, 4), s))

    def signal(sem, devices):
        for dev in devices:
            pl.semaphore_signal(sem, inc=1, device_id=dev, device_id_type=MESH)

    signal(barrier, (sib, to_right, to_left, *z_next, *x_next))

    col = lax.broadcasted_iota(jnp.int32, (D, D), 1)

    def weight(index):
        return jnp.sum(jnp.where(col == index, wt[...], 0.0), -1, keepdims=True)

    def state(head):
        kk = k[:, cols(head)].astype(jnp.float32)
        kn = (kk * lax.rsqrt(jnp.mean(kk * kk, -1, keepdims=True) + EPS)).astype(jnp.bfloat16)
        return lax.dot_general(
            kn, v[:, cols(head)], (((0,), (0,)), ((), ())), preferred_element_type=jnp.float32
        )

    def attend(first, last):
        @pl.loop(first, last)
        def _(j):
            for i in range(CH):
                h = j * CH + i
                qq = q[:, cols(h)]
                scores = lax.dot_general(
                    qq, k[:, cols(h)], (((1,), (1,)), ((), ())), preferred_element_type=jnp.float32
                )
                scores = scores + bias[...]
                top = jnp.max(scores, -1, keepdims=True)
                p = jnp.exp((scores - top) * (1.0 / math.sqrt(D)))
                total = jnp.sum(p, -1, keepdims=True)
                mix = jnp.dot(p.astype(jnp.bfloat16), v[:, cols(h)], preferred_element_type=jnp.float32)
                loc[:, cols(h)] = mix * (weight(h) / total)
                q32 = qq.astype(jnp.float32)
                r = lax.rsqrt(jnp.mean(q32 * q32, -1, keepdims=True) + EPS)
                qs[0, :, cols(h)] = (q32 * (r * weight(HEADS + h))).astype(jnp.bfloat16)
                qs[1, :, cols(h)] = (q32 * (r * weight(2 * HEADS + h))).astype(jnp.bfloat16)

    def rows(chunk, first=0, count=CR):
        return pl.ds(pl.multiple_of(chunk * CR + first, PR), count)

    def sib_copy(j, yc):
        return send(sib_out.at[rows(yc)], sib_in.at[rows(yc)], sib_s.at[j], sib_r.at[j], sib)


    y_copies = [send(y_out.at[i], y_in.at[i], y_s.at[i], y_r.at[i], across[i][0]) for i in range(3)]

    def z_copy(step):
        dst_z = lax.rem(z + step, NZ)
        return send(
            z_out.at[pl.ds(pl.multiple_of(dst_z * PR, PR), PR)],
            z_in.at[step],
            z_s.at[step],
            z_r.at[step],
            z_peer(step),
        )

    def x_copy(src_f, dst_f):
        return send(x_out, x_in.at[src_f], x_s.at[dst_f], x_r.at[src_f], (dst_f, s))

    sending = f < 3

    def states(j, half):
        with scope("st"):
            load(j, half, 0).wait()
            load(j, half, 1).wait()
            yc = chunk_at(j)
            side = (1 - c, c)[half]
            for i in range(CH):
                value = state(side * HALF + yc * CH + i)
                span = pl.ds(pl.multiple_of(yc * CR + i * D, D), D)
                if half == 0:
                    sib_out[span] = value.astype(jnp.bfloat16)
                else:
                    part[span] = value

    def add_sib(j):
        yc = chunk_at(j)
        with scope("sw"):
            sib_copy(j, yc).wait_recv()
        return part[rows(yc)] + sib_in[rows(yc)].astype(jnp.float32)

    def send_y(j):
        y_out[j] = add_sib(j).astype(jnp.bfloat16)
        y_copies[j].start()

    @pl.when(sending)
    def _():
        states(0, 0)

    with scope("barrier"):
        pl.semaphore_wait(barrier, 7)
    signal(step_sem.at[0], z_next)
    signal(step_sem.at[3], (to_right, to_left))
    signal(step_sem.at[4], x_next)

    @pl.when(sending)
    def _():
        sib_copy(0, chunk_at(0)).start()
        states(0, 1)
        states(1, 0)
        sib_copy(1, chunk_at(1)).start()
        states(1, 1)

    with scope("x1"):
        pl.semaphore_wait(step_sem.at[3], 2)

    @pl.when(sending)
    def _():
        send_y(0)

    with scope("b1"):
        pl.semaphore_wait(step_sem.at[0], 2)
    signal(step_sem.at[1], z_next)

    @pl.when(sending)
    def _():
        states(2, 0)
        sib_copy(2, chunk_at(2)).start()
        states(2, 1)
        send_y(1)
        states(3, 0)
        sib_copy(3, chunk_at(3)).start()
        states(3, 1)
        send_y(2)

    with scope("b2"):
        pl.semaphore_wait(step_sem.at[1], 2)
    signal(step_sem.at[2], z_next)

    @pl.when(sending)
    def _():
        part[rows(y)] = add_sib(3)

    @pl.when(jnp.logical_not(sending))
    def _():
        for j in range(NY):
            for half in range(2):
                load(j, half, 0).wait()
                load(j, half, 1).wait()

    for cp in small:
        cp.wait()
    row = lax.broadcasted_iota(jnp.int32, (D, D), 0)
    floor = jnp.full((D, D), 0, jnp.int32)
    start = 0
    for i in range(4):
        low = jnp.maximum(start - wback[0, i], 0)
        floor = jnp.where(row >= start, low, floor)
        start = start + flen[0, i]
    bias[...] = jnp.where((col <= row) & (col >= floor), 0.0, -jnp.inf)
    scale1 = 1.0 / math.sqrt(D * block_tokens)
    scale2 = 1.0 / math.sqrt(D * 2 * block_tokens)
    wrows[...] = jnp.zeros_like(wrows)
    wrows[0:HEADS] = lw[0]
    wrows[HEADS : 2 * HEADS] = jnp.where(f == 2, lw[2] * scale2, lw[1] * scale1)
    wrows[2 * HEADS : 3 * HEADS] = lw[2] * scale2
    wt[...] = jnp.transpose(wrows[...])

    with scope("att0"):
        attend(0, 1)

    with scope("att1"):
        attend(1, 4)
    with scope("b3"):
        pl.semaphore_wait(step_sem.at[2], 2)
        pl.semaphore_wait(step_sem.at[4], 2)

    @pl.when(sending)
    def _():
        with scope("yw2"):
            for cp in y_copies:
                cp.wait_recv()
        total = part[rows(y)]
        for i in range(3):
            total = total + y_in[i].astype(jnp.float32)
        part[rows(y)] = total
        z_out[...] = total.astype(jnp.bfloat16)
        for i in (4, 3, 5, 2, 6, 1, 7):
            z_copy(i).start()

    with scope("att2"):
        attend(4, 8)

    @pl.when(sending)
    def _():
        total = part[pl.ds(pl.multiple_of(y * CR + z * PR, PR), PR)]
        for i in range(1, NZ):
            with scope("zw"):
                z_copy(i).wait_recv()
            total = total + z_in[i].astype(jnp.float32)
        x_out[...] = total.astype(jnp.bfloat16)

        for src in range(3):

            @pl.when(f == src)
            def _():
                for dst in range(3, src, -1):
                    x_copy(src, dst).start()

    chunk = c * NY + y
    piece = pl.ds(pl.multiple_of(chunk * CR + z * PR, PR), PR)

    @pl.when(f == 1)
    def _():
        with scope("xw"):
            x_copy(0, 1).wait_recv()
        lev[0, piece] = x_in[0]

    @pl.when(f == 2)
    def _():
        with scope("xw"):
            x_copy(0, 2).wait_recv()
        with scope("xw"):
            x_copy(1, 2).wait_recv()
        lev[0, piece] = (x_in[0].astype(jnp.float32) + x_in[1].astype(jnp.float32)).astype(jnp.bfloat16)

    @pl.when(f == 3)
    def _():
        for src in range(3):
            with scope("xw"):
                x_copy(src, 3).wait_recv()
        lev[0, piece] = x_in[2]
        lev[1, piece] = (x_in[0].astype(jnp.float32) + x_in[1].astype(jnp.float32)).astype(jnp.bfloat16)

    def gather(n):
        def move(at_row, count, ssem, rsem, dev):
            span = pl.ds(pl.multiple_of(at_row, PR), count)
            return Group(
                [send(lev.at[m, span], lev.at[m, span], ssem.at[m], rsem.at[m], dev) for m in range(n)]
            )

        def at_piece(yc, step):
            return (c * NY + yc) * CR + lax.rem(z + NZ - step, NZ) * PR

        def gz(step):
            return move(at_piece(y, 0), PR, gz_s.at[step], gz_r.at[step], z_peer(step))

        def gy(i, step):
            return move(at_piece(y, step), PR, gy_s.at[i, step], gy_r.at[i, step], across[i][0])

        source = (opp, left, right)

        def share(i, step):
            return move(at_piece(source[i], step), PR, gs_s.at[i, step], gs_r.at[i, step], sib)

        def share_own():
            return move((c * NY + y) * CR, CR, gs_s.at[3, 0], gs_r.at[3, 0], sib)

        def read(chunk_index):
            for i in range(CH):
                h = chunk_index * CH + i
                value = loc[:, cols(h)]
                for m in range(n):
                    value = value + jnp.dot(
                        qs[m, :, cols(h)], lev[m, pl.ds(pl.multiple_of(h * D, D), D)], preferred_element_type=jnp.float32
                    )
                out[:, cols(h)] = value.astype(jnp.bfloat16)

        def forward(*steps):
            for step in steps:
                if step:
                    with scope("gzw%d" % step):
                        gz(step).wait_recv()
                for i in range(3):
                    gy(i, step).start()

        def pass_on(*steps):
            for step in steps:
                for i in range(3):
                    with scope("gyw%d%d" % (i, step)):
                        gy(i, step).wait_recv()
                    share(i, step).start()

        gz(1).start()
        gz(7).start()
        forward(0)
        for step in (4, 2, 6, 3, 5):
            gz(step).start()
        forward(1, 7, 2, 6, 3, 5, 4)
        share_own().start()
        read(c * NY + y)
        pass_on(0, 1, 7, 2, 6)
        with scope("sw0"):
            share_own().wait_recv()
        read((1 - c) * NY + y)
        pass_on(3, 5, 4)
        for yc in source:
            read(c * NY + yc)
        for i, yc in enumerate(source):
            for step in ORDER:
                with scope("gsw%d%d" % (i, step)):
                    share(i, step).wait_recv()
            read((1 - c) * NY + yc)
        for step in range(NZ):
            if step:
                with scope("ws"):
                    gz(step).wait_send()
            for i in range(3):
                gy(i, step).wait_send()
                share(i, step).wait_send()
        share_own().wait_send()

    @pl.when(f == 0)
    def _():
        @pl.loop(0, 2 * NY)
        def _(j):
            out[:, cols(j * CH, CH)] = loc[:, cols(j * CH, CH)].astype(jnp.bfloat16)

    @pl.when((f == 1) | (f == 2))
    def _():
        gather(1)

    @pl.when(f == 3)
    def _():
        gather(2)

    @pl.when(sending)
    def _():
        for j in range(NY):
            with scope('tail'):
                sib_copy(j, chunk_at(j)).wait_send()
        for cp in y_copies:
            cp.wait_send()
        for i in range(1, NZ):
            z_copy(i).wait_send()
        for src in range(3):

            @pl.when(f == src)
            def _():
                for dst in range(3, src, -1):
                    x_copy(src, dst).wait_send()


def body(space_count, queries, keys, values, level_weight, frame_len, window_back):
    tok, width = queries.shape
    f32, bf16 = jnp.float32, jnp.bfloat16
    dma = pltpu.SemaphoreType.DMA
    anyspec = pl.BlockSpec(memory_space=pl.ANY)
    return pl.pallas_call(
        functools.partial(kernel, tok * space_count),
        out_shape=pltpu.VMEM((tok, width), bf16),
        in_specs=[anyspec] * 6,
        out_specs=pl.BlockSpec(memory_space=pltpu.VMEM),
        scratch_shapes=[
            pltpu.SMEM((1, 4), jnp.int32),
            pltpu.SMEM((1, 4), jnp.int32),
            pltpu.VMEM(level_weight.shape, f32),
            pltpu.VMEM((tok, width), bf16),
            pltpu.VMEM((tok, width), bf16),
            pltpu.VMEM((tok, width), bf16),
            pltpu.VMEM((D, D), f32),
            pltpu.VMEM((D, D), f32),
            pltpu.VMEM((D, D), f32),
            pltpu.VMEM((tok, width), f32),
            pltpu.VMEM((2, tok, width), bf16),
            pltpu.VMEM((HALF * D, D), f32),
            pltpu.VMEM((HALF * D, D), bf16),
            pltpu.VMEM((HALF * D, D), bf16),
            pltpu.VMEM((3, CR, D), bf16),
            pltpu.VMEM((3, CR, D), bf16),
            pltpu.VMEM((CR, D), bf16),
            pltpu.VMEM((NZ, PR, D), bf16),
            pltpu.VMEM((PR, D), bf16),
            pltpu.VMEM((3, PR, D), bf16),
            pltpu.VMEM((2, HEADS * D, D), bf16),
            dma((NY, 2, 2)),
            dma((4,)),
            pltpu.SemaphoreType.REGULAR((5,)),
            dma((NY,)),
            dma((NY,)),
            dma((3,)),
            dma((3,)),
            dma((NZ,)),
            dma((NZ,)),
            dma((4,)),
            dma((4,)),
            dma((NZ, 2)),
            dma((NZ, 2)),
            dma((3, NZ, 2)),
            dma((3, NZ, 2)),
            dma((4, NZ, 2)),
            dma((4, NZ, 2)),
        ],
        compiler_params=pltpu.CompilerParams(collective_id=0, has_side_effects=True),
    )(frame_len, window_back, level_weight, queries, keys, values)


def solution(mesh):
    return jax.shard_map(
        functools.partial(body, mesh.shape["space"]),
        mesh=mesh,
        in_specs=(
            P(("frame", "space"), None),
            P(("frame", "space"), None),
            P(("frame", "space"), None),
            P(None, None, ("frame", "space")),
            P(("frame", "space"), None),
            P(("frame", "space"), None),
        ),
        out_specs=P(("frame", "space"), None),
        check_vma=False,
    )
```

```python
import contextlib
import functools
import math

import jax
import jax.numpy as jnp
from jax import lax
from jax.experimental import pallas as pl
from jax.experimental.pallas import tpu as pltpu
from jax.sharding import PartitionSpec as P

MESH = pl.DeviceIdType.MESH
HEADS = 24
HALF = 12
D = 128
EPS = 1e-06
NY = 4
NZ = 8
CH = 3
CR = CH * D
PR = CR // NZ
ORDER = (0, 1, 7, 2, 6, 3, 5, 4)
DELIVER = (0, 1, 7, 4, 2, 6, 3, 5)


def scope(name):
    return contextlib.nullcontext()


def kernel(
    block_tokens,
    flen_hbm,
    wback_hbm,
    lw_hbm,
    q_hbm,
    k_hbm,
    v_hbm,
    out,
    flen,
    wback,
    lw,
    q,
    k,
    v,
    bias,
    wrows,
    wt,
    loc,
    qs,
    part,
    sib_out,
    sib_in,
    y_out,
    y_in,
    z_out,
    z_in,
    x_out,
    lev,
    load_sem,
    misc_sem,
    step_sem,
    sib_s,
    sib_r,
    y_s,
    y_r,
    z_s,
    z_r,
    d_s,
    gz_r,
    gy_s,
    gy_r,
    gs_s,
    gs_r,
):
    f = lax.axis_index("frame")
    s = lax.axis_index("space")
    c = lax.rem(s, 2)
    y = lax.rem(s // 2, NY)
    z = s // (2 * NY)
    right = lax.rem(y + 1, NY)
    left = lax.rem(y + NY - 1, NY)
    opp = lax.rem(y + 2, NY)

    def at(zz, yy, cc):
        return (zz * NY + yy) * 2 + cc

    sib = (f, at(z, y, 1 - c))
    to_right = (f, at(z, right, c))
    to_left = (f, at(z, left, c))
    to_opp = (f, at(z, opp, c))
    across = ((to_opp, opp), (to_right, right), (to_left, left))

    def z_peer(step, ff=f):
        return (ff, at(lax.rem(z + step, NZ), y, c))

    def cols(head, count=1):
        return pl.ds(pl.multiple_of(head * D, D), count * D)

    def send(src, dst, ssem, rsem, dev):
        return pltpu.make_async_remote_copy(
            src_ref=src, dst_ref=dst, send_sem=ssem, recv_sem=rsem, device_id=dev, device_id_type=MESH
        )

    class Group:
        def __init__(self, copies):
            self.copies = copies

        def start(self):
            for cp in self.copies:
                cp.start()

        def wait_recv(self):
            for cp in self.copies:
                cp.wait_recv()

        def wait_send(self):
            for cp in self.copies:
                cp.wait_send()

    def chunk_at(j):
        return (opp, right, left, y)[j]

    def load(j, half, which):
        src, dst = ((k_hbm, k), (v_hbm, v))[which]
        side = (1 - c, c)[half]
        span = cols(side * HALF + chunk_at(j) * CH, CH)
        return pltpu.make_async_copy(src.at[:, span], dst.at[:, span], load_sem.at[j, half, which])

    for j in range(NY):
        for half in range(2):
            for which in range(2):
                load(j, half, which).start()
    small = [
        pltpu.make_async_copy(src, dst, misc_sem.at[i])
        for i, (src, dst) in enumerate(((flen_hbm, flen), (wback_hbm, wback), (lw_hbm, lw), (q_hbm, q)))
    ]
    for cp in small:
        cp.start()

    barrier = pltpu.get_barrier_semaphore()
    z_next = (z_peer(1), z_peer(NZ - 1))
    x_next = ((lax.rem(f + 1, 4), s), (lax.rem(f + 3, 4), s))

    def signal(sem, devices):
        for dev in devices:
            pl.semaphore_signal(sem, inc=1, device_id=dev, device_id_type=MESH)

    signal(barrier, (sib, to_right, to_left, *z_next, *x_next))

    col = lax.broadcasted_iota(jnp.int32, (D, D), 1)

    def weight(index):
        return jnp.sum(jnp.where(col == index, wt[...], 0.0), -1, keepdims=True)

    def state(head):
        kk = k[:, cols(head)].astype(jnp.float32)
        kn = (kk * lax.rsqrt(jnp.mean(kk * kk, -1, keepdims=True) + EPS)).astype(jnp.bfloat16)
        return lax.dot_general(
            kn, v[:, cols(head)], (((0,), (0,)), ((), ())), preferred_element_type=jnp.float32
        )

    def attend(first, last):
        @pl.loop(first, last)
        def _(j):
            for i in range(CH):
                h = j * CH + i
                qq = q[:, cols(h)]
                scores = lax.dot_general(
                    qq, k[:, cols(h)], (((1,), (1,)), ((), ())), preferred_element_type=jnp.float32
                )
                scores = scores + bias[...]
                top = jnp.max(scores, -1, keepdims=True)
                p = jnp.exp((scores - top) * (1.0 / math.sqrt(D)))
                total = jnp.sum(p, -1, keepdims=True)
                mix = jnp.dot(p.astype(jnp.bfloat16), v[:, cols(h)], preferred_element_type=jnp.float32)
                loc[:, cols(h)] = mix * (weight(h) / total)
                q32 = qq.astype(jnp.float32)
                r = lax.rsqrt(jnp.mean(q32 * q32, -1, keepdims=True) + EPS)
                qs[0, :, cols(h)] = (q32 * (r * weight(HEADS + h))).astype(jnp.bfloat16)
                qs[1, :, cols(h)] = (q32 * (r * weight(2 * HEADS + h))).astype(jnp.bfloat16)

    def rows(chunk, first=0, count=CR):
        return pl.ds(pl.multiple_of(chunk * CR + first, PR), count)

    def sib_copy(j, yc):
        return send(sib_out.at[rows(yc)], sib_in.at[rows(yc)], sib_s.at[j], sib_r.at[j], sib)


    y_copies = [send(y_out.at[i], y_in.at[i], y_s.at[i], y_r.at[i], across[i][0]) for i in range(3)]

    summing = c == f
    slot = jnp.where(f == 2, 0, f)

    def z_copy(step, source=slot):
        at_row = pl.multiple_of(lax.rem(z + step, NZ) * PR, PR)
        return send(
            z_out.at[pl.ds(at_row, PR)],
            z_in.at[source, step],
            z_s.at[step],
            z_r.at[source, step],
            z_peer(step, jnp.where(f == 2, 2, c)),
        )

    chunk = c * NY + y
    piece = pl.ds(pl.multiple_of(chunk * CR + z * PR, PR), PR)

    def deliver(step, k, target, m):
        return send(x_out.at[k], lev.at[m, piece], d_s.at[target - 1, step], gz_r.at[m, step], z_peer(step, target))

    def deliveries():
        return (
            ((f < 2) & summing, [(step, 1, target, target - 2) for step in DELIVER for target in (2, 3)]),
            ((f == 0) & summing, [(step, 0, 1, 0) for step in DELIVER]),
            ((f == 1) & summing, [(step, 0, 1, 0) for step in DELIVER if step]),
            (f == 2, [(step, 0, 3, 0) for step in DELIVER]),
        )

    sending = f < 3

    def states(j, half):
        with scope("st"):
            load(j, half, 0).wait()
            load(j, half, 1).wait()
            yc = chunk_at(j)
            side = (1 - c, c)[half]
            for i in range(CH):
                value = state(side * HALF + yc * CH + i)
                span = pl.ds(pl.multiple_of(yc * CR + i * D, D), D)
                if half == 0:
                    sib_out[span] = value.astype(jnp.bfloat16)
                else:
                    part[span] = value

    def add_sib(j):
        yc = chunk_at(j)
        with scope("sw"):
            sib_copy(j, yc).wait_recv()
        return part[rows(yc)] + sib_in[rows(yc)].astype(jnp.float32)

    def send_y(j):
        y_out[j] = add_sib(j).astype(jnp.bfloat16)
        y_copies[j].start()

    @pl.when(sending)
    def _():
        states(0, 0)

    with scope("barrier"):
        pl.semaphore_wait(barrier, 7)
    signal(step_sem.at[0], z_next)
    signal(step_sem.at[3], (to_right, to_left))

    @pl.when(sending)
    def _():
        sib_copy(0, chunk_at(0)).start()
        states(0, 1)
        states(1, 0)
        sib_copy(1, chunk_at(1)).start()
        states(1, 1)

    with scope("x1"):
        pl.semaphore_wait(step_sem.at[3], 2)

    @pl.when(sending)
    def _():
        send_y(0)

    with scope("b1"):
        pl.semaphore_wait(step_sem.at[0], 2)
    signal(step_sem.at[1], z_next)

    @pl.when(sending)
    def _():
        states(2, 0)
        sib_copy(2, chunk_at(2)).start()
        states(2, 1)
        send_y(1)
        states(3, 0)
        sib_copy(3, chunk_at(3)).start()
        states(3, 1)
        send_y(2)

    with scope("b2"):
        pl.semaphore_wait(step_sem.at[1], 2)
    signal(step_sem.at[2], z_next)

    @pl.when(sending)
    def _():
        part[rows(y)] = add_sib(3)

    @pl.when(jnp.logical_not(sending))
    def _():
        for j in range(NY):
            for half in range(2):
                load(j, half, 0).wait()
                load(j, half, 1).wait()

    for cp in small:
        cp.wait()
    row = lax.broadcasted_iota(jnp.int32, (D, D), 0)
    floor = jnp.full((D, D), 0, jnp.int32)
    start = 0
    for i in range(4):
        low = jnp.maximum(start - wback[0, i], 0)
        floor = jnp.where(row >= start, low, floor)
        start = start + flen[0, i]
    bias[...] = jnp.where((col <= row) & (col >= floor), 0.0, -jnp.inf)
    scale1 = 1.0 / math.sqrt(D * block_tokens)
    scale2 = 1.0 / math.sqrt(D * 2 * block_tokens)
    wrows[...] = jnp.zeros_like(wrows)
    wrows[0:HEADS] = lw[0]
    wrows[HEADS : 2 * HEADS] = jnp.where(f == 2, lw[2] * scale2, lw[1] * scale1)
    wrows[2 * HEADS : 3 * HEADS] = lw[2] * scale2
    wt[...] = jnp.transpose(wrows[...])

    with scope("att0"):
        attend(0, 1)
    with scope("b3"):
        pl.semaphore_wait(step_sem.at[2], 2)
    signal(step_sem.at[4], z_next)
    with scope("att1"):
        attend(1, 4)
    with scope("b4"):
        pl.semaphore_wait(step_sem.at[4], 2)
    signal(step_sem.at[5], x_next)

    @pl.when(sending)
    def _():
        with scope("yw2"):
            for cp in y_copies:
                cp.wait_recv()
        total = part[rows(y)]
        for i in range(3):
            total = total + y_in[i].astype(jnp.float32)
        part[rows(y)] = total
        z_out[...] = total.astype(jnp.bfloat16)
        for i in (4, 3, 5, 2, 6, 1, 7):
            z_copy(i).start()

        @pl.when((f < 2) & jnp.logical_not(summing))
        def _():
            z_copy(0).start()

    with scope("att2"):
        attend(4, 8)

    with scope("b5"):
        pl.semaphore_wait(step_sem.at[5], 2)

    @pl.when((f == 2) | ((f < 2) & summing))
    def _():
        total = part[pl.ds(pl.multiple_of(y * CR + z * PR, PR), PR)]
        for i in range(1, NZ):
            with scope("zw"):
                z_copy(i).wait_recv()
            total = total + z_in[slot, i].astype(jnp.float32)

        @pl.when(f == 2)
        def _():
            x_out[0] = total.astype(jnp.bfloat16)

        @pl.when(f < 2)
        def _():
            across_sum = jnp.zeros_like(total)
            for i in range(NZ):
                with scope("zc"):
                    z_copy(i, 1 - slot).wait_recv()
                across_sum = across_sum + z_in[1 - slot, i].astype(jnp.float32)
            x_out[1] = (total + across_sum).astype(jnp.bfloat16)
            x_out[0] = jnp.where(f == 0, total, across_sum).astype(jnp.bfloat16)

    for who, what in deliveries():

        @pl.when(who)
        def _():
            for args in what:
                deliver(*args).start()

    @pl.when((f == 1) & summing)
    def _():
        lev[0, piece] = x_out[0]

    def gather(n):
        def move(m, at_row, count, ssem, rsem, dev):
            span = pl.ds(pl.multiple_of(at_row, PR), count)
            return send(lev.at[m, span], lev.at[m, span], ssem, rsem, dev)

        def at_piece(yc, step):
            return (c * NY + yc) * CR + lax.rem(z + NZ - step, NZ) * PR

        def gz(m, step):
            return move(m, at_piece(y, step), PR, d_s.at[m, step], gz_r.at[m, step], sib)

        def gy(m, i, step):
            return move(m, at_piece(y, step), PR, gy_s.at[m, i, step], gy_r.at[m, i, step], across[i][0])

        source = (opp, left, right)

        def share(m, i, step):
            return move(m, at_piece(source[i], step), PR, gs_s.at[m, i, step], gs_r.at[m, i, step], sib)

        def share_own(m):
            return move(m, (c * NY + y) * CR, CR, gs_s.at[m, 3, 0], gs_r.at[m, 3, 0], sib)

        def read(m, chunk_index, last=True):
            for i in range(CH):
                h = chunk_index * CH + i
                value = loc[:, cols(h)] + jnp.dot(
                    qs[m, :, cols(h)], lev[m, pl.ds(pl.multiple_of(h * D, D), D)], preferred_element_type=jnp.float32
                )
                if last:
                    out[:, cols(h)] = value.astype(jnp.bfloat16)
                else:
                    loc[:, cols(h)] = value

        def forward(m, *steps):
            for step in steps:
                with scope("gzw%d%d" % (m, step)):
                    if step == 0 and n == 1:

                        @pl.when(jnp.logical_not((f == 1) & summing))
                        def _():
                            gz(m, step).wait_recv()

                    else:
                        gz(m, step).wait_recv()
                for i in range(3):
                    gy(m, i, step).start()

        def pass_on(m, *steps):
            for step in steps:
                for i in range(3):
                    with scope("gyw%d%d%d" % (m, i, step)):
                        gy(m, i, step).wait_recv()
                    share(m, i, step).start()

        for m in range(n):
            forward(m, *ORDER)
            share_own(m).start()
        m = n - 1
        if n == 2:
            pass_on(0, *ORDER)
            for yc in (y, *source):
                read(0, c * NY + yc, False)
        else:
            read(0, c * NY + y)
        pass_on(m, *ORDER)
        for k in range(n):
            with scope("sw%d" % k):
                share_own(k).wait_recv()
            read(k, (1 - c) * NY + y, k == m)
        if n == 2:
            for i, yc in enumerate(source):
                for step in ORDER:
                    with scope("gsw0%d%d" % (i, step)):
                        share(0, i, step).wait_recv()
                read(0, (1 - c) * NY + yc, False)
            read(m, c * NY + y)
        for yc in source:
            read(m, c * NY + yc)
        for i, yc in enumerate(source):
            for step in ORDER:
                with scope("gsw%d%d%d" % (m, i, step)):
                    share(m, i, step).wait_recv()
            read(m, (1 - c) * NY + yc)
        for m in range(n):
            for step in range(NZ):
                for i in range(3):
                    gy(m, i, step).wait_send()
                    share(m, i, step).wait_send()
            share_own(m).wait_send()

    @pl.when(f == 0)
    def _():
        @pl.loop(0, 2 * NY)
        def _(j):
            out[:, cols(j * CH, CH)] = loc[:, cols(j * CH, CH)].astype(jnp.bfloat16)

    @pl.when((f == 1) | (f == 2))
    def _():
        gather(1)

    @pl.when(f == 3)
    def _():
        gather(2)

    @pl.when(sending)
    def _():
        for j in range(NY):
            with scope('tail'):
                sib_copy(j, chunk_at(j)).wait_send()
        for cp in y_copies:
            cp.wait_send()
        for i in range(1, NZ):
            z_copy(i).wait_send()

        @pl.when((f < 2) & jnp.logical_not(summing))
        def _():
            z_copy(0).wait_send()

    for who, what in deliveries():

        @pl.when(who)
        def _():
            for args in what:
                deliver(*args).wait_send()


def body(space_count, queries, keys, values, level_weight, frame_len, window_back):
    tok, width = queries.shape
    f32, bf16 = jnp.float32, jnp.bfloat16
    dma = pltpu.SemaphoreType.DMA
    anyspec = pl.BlockSpec(memory_space=pl.ANY)
    return pl.pallas_call(
        functools.partial(kernel, tok * space_count),
        out_shape=pltpu.VMEM((tok, width), bf16),
        in_specs=[anyspec] * 6,
        out_specs=pl.BlockSpec(memory_space=pltpu.VMEM),
        scratch_shapes=[
            pltpu.SMEM((1, 4), jnp.int32),
            pltpu.SMEM((1, 4), jnp.int32),
            pltpu.VMEM(level_weight.shape, f32),
            pltpu.VMEM((tok, width), bf16),
            pltpu.VMEM((tok, width), bf16),
            pltpu.VMEM((tok, width), bf16),
            pltpu.VMEM((D, D), f32),
            pltpu.VMEM((D, D), f32),
            pltpu.VMEM((D, D), f32),
            pltpu.VMEM((tok, width), f32),
            pltpu.VMEM((2, tok, width), bf16),
            pltpu.VMEM((HALF * D, D), f32),
            pltpu.VMEM((HALF * D, D), bf16),
            pltpu.VMEM((HALF * D, D), bf16),
            pltpu.VMEM((3, CR, D), bf16),
            pltpu.VMEM((3, CR, D), bf16),
            pltpu.VMEM((CR, D), bf16),
            pltpu.VMEM((2, NZ, PR, D), bf16),
            pltpu.VMEM((2, PR, D), bf16),
            pltpu.VMEM((2, HEADS * D, D), bf16),
            dma((NY, 2, 2)),
            dma((4,)),
            pltpu.SemaphoreType.REGULAR((6,)),
            dma((NY,)),
            dma((NY,)),
            dma((3,)),
            dma((3,)),
            dma((NZ,)),
            dma((2, NZ)),
            dma((3, NZ)),
            dma((2, NZ)),
            dma((2, 3, NZ)),
            dma((2, 3, NZ)),
            dma((2, 4, NZ)),
            dma((2, 4, NZ)),
        ],
        compiler_params=pltpu.CompilerParams(collective_id=0, has_side_effects=True),
    )(frame_len, window_back, level_weight, queries, keys, values)


def solution(mesh):
    return jax.shard_map(
        functools.partial(body, mesh.shape["space"]),
        mesh=mesh,
        in_specs=(
            P(("frame", "space"), None),
            P(("frame", "space"), None),
            P(("frame", "space"), None),
            P(None, None, ("frame", "space")),
            P(("frame", "space"), None),
            P(("frame", "space"), None),
        ),
        out_specs=P(("frame", "space"), None),
        check_vma=False,
    )
```

```python
import contextlib
import functools
import math

import jax
import jax.numpy as jnp
from jax import lax
from jax.experimental import pallas as pl
from jax.experimental.pallas import tpu as pltpu
from jax.sharding import PartitionSpec as P

MESH = pl.DeviceIdType.MESH
HEADS = 24
HALF = 12
D = 128
EPS = 1e-06
NY = 4
NZ = 8
CH = 3
CR = CH * D
PR = CR // NZ
PA = 32
PB = PR - PA
ORDER = (0, 1, 7, 2, 6, 3, 5, 4)
DELIVER = (0, 4, 1, 3, 5, 7, 2, 6)
GROUPS = ((0,), (1, 7), (2, 6), (3, 5, 4))
GROUP = (0, 1, 2, 3, 3, 3, 2, 1)


def scope(name):
    return contextlib.nullcontext()


def kernel(
    block_tokens,
    flen_hbm,
    wback_hbm,
    lw_hbm,
    q_hbm,
    k_hbm,
    v_hbm,
    out,
    flen,
    wback,
    lw,
    q,
    k,
    v,
    bias,
    wrows,
    wt,
    loc,
    qs,
    part,
    sib_out,
    sib_in,
    y_out,
    y_in,
    z_out,
    z_in,
    x_out,
    lev,
    load_sem,
    misc_sem,
    step_sem,
    sent,
    sib_r,
    y_r,
    z_r,
    gz_r,
    gb_r,
    gy_r,
    zb_r,
    gs_r,
):
    f = lax.axis_index("frame")
    s = lax.axis_index("space")
    c = lax.rem(s, 2)
    y = lax.rem(s // 2, NY)
    z = s // (2 * NY)
    right = lax.rem(y + 1, NY)
    left = lax.rem(y + NY - 1, NY)
    opp = lax.rem(y + 2, NY)

    def at(zz, yy, cc):
        return (zz * NY + yy) * 2 + cc

    sib = (f, at(z, y, 1 - c))
    to_right = (f, at(z, right, c))
    to_left = (f, at(z, left, c))
    to_opp = (f, at(z, opp, c))
    across = ((to_opp, opp), (to_right, right), (to_left, left))

    def z_peer(step, ff=f):
        return (ff, at(lax.rem(z + step, NZ), y, c))

    def cols(head, count=1):
        return pl.ds(pl.multiple_of(head * D, D), count * D)

    def send(src, dst, ssem, rsem, dev):
        return pltpu.make_async_remote_copy(
            src_ref=src, dst_ref=dst, send_sem=ssem, recv_sem=rsem, device_id=dev, device_id_type=MESH
        )

    class Group:
        def __init__(self, copies):
            self.copies = copies

        def start(self):
            for cp in self.copies:
                cp.start()

        def wait_recv(self):
            for cp in self.copies:
                cp.wait_recv()

        def wait_send(self):
            for cp in self.copies:
                cp.wait_send()

    def chunk_at(j):
        return (opp, right, left, y)[j]

    def load(j, half, which):
        src, dst = ((k_hbm, k), (v_hbm, v))[which]
        side = (1 - c, c)[half]
        span = cols(side * HALF + chunk_at(j) * CH, CH)
        return pltpu.make_async_copy(src.at[:, span], dst.at[:, span], load_sem.at[j, half])

    def loaded(j, half):
        both = k.at[:, pl.ds(0, 2 * CR)]
        pltpu.make_async_copy(k_hbm.at[:, pl.ds(0, 2 * CR)], both, load_sem.at[j, half]).wait()

    for j in range(NY):
        for half in range(2):
            for which in range(2):
                load(j, half, which).start()
    small = [
        pltpu.make_async_copy(src, dst, misc_sem.at[i])
        for i, (src, dst) in enumerate(((flen_hbm, flen), (wback_hbm, wback), (lw_hbm, lw), (q_hbm, q)))
    ]
    for cp in small:
        cp.start()

    barrier = pltpu.get_barrier_semaphore()
    z_next = (z_peer(1), z_peer(NZ - 1))
    x_next = ((lax.rem(f + 1, 4), s), (lax.rem(f + 3, 4), s))

    def signal(sem, devices):
        for dev in devices:
            pl.semaphore_signal(sem, inc=1, device_id=dev, device_id_type=MESH)

    signal(barrier, (sib, to_right, to_left, *z_next, *x_next))

    col = lax.broadcasted_iota(jnp.int32, (D, D), 1)

    def weight(index):
        return jnp.sum(jnp.where(col == index, wt[...], 0.0), -1, keepdims=True)

    def state(head):
        kk = k[:, cols(head)].astype(jnp.float32)
        kn = (kk * lax.rsqrt(jnp.mean(kk * kk, -1, keepdims=True) + EPS)).astype(jnp.bfloat16)
        return lax.dot_general(
            kn, v[:, cols(head)], (((0,), (0,)), ((), ())), preferred_element_type=jnp.float32
        )

    def attend(first, last):
        @pl.loop(first, last)
        def _(j):
            for i in range(CH):
                h = j * CH + i
                qq = q[:, cols(h)]
                scores = lax.dot_general(
                    qq, k[:, cols(h)], (((1,), (1,)), ((), ())), preferred_element_type=jnp.float32
                )
                scores = scores + bias[...]
                top = jnp.max(scores, -1, keepdims=True)
                p = jnp.exp((scores - top) * (1.0 / math.sqrt(D)))
                total = jnp.sum(p, -1, keepdims=True)
                mix = jnp.dot(p.astype(jnp.bfloat16), v[:, cols(h)], preferred_element_type=jnp.float32)
                loc[:, cols(h)] = mix * (weight(h) / total)
                q32 = qq.astype(jnp.float32)
                r = lax.rsqrt(jnp.mean(q32 * q32, -1, keepdims=True) + EPS)
                qs[0, :, cols(h)] = (q32 * (r * weight(HEADS + h))).astype(jnp.bfloat16)
                qs[1, :, cols(h)] = (q32 * (r * weight(2 * HEADS + h))).astype(jnp.bfloat16)

    def group(count, sem):
        whole = sib_in.at[pl.ds(0, count)]
        return send(whole, whole, sem, sem, sib)

    def rows(chunk, first=0, count=CR):
        return pl.ds(pl.multiple_of(chunk * CR + first, PR), count)

    def sib_copy(j, yc):
        return send(sib_out.at[rows(yc)], sib_in.at[rows(yc)], sent.at[0], sib_r.at[j], sib)


    y_copies = [send(y_out.at[i], y_in.at[i], sent.at[1], y_r.at[0], across[i][0]) for i in range(3)]

    summing = c == f
    slot = jnp.where(f == 2, 0, f)

    def z_copy(step, source=slot):
        at_row = pl.multiple_of(lax.rem(z + step, NZ) * PR, PR)
        return send(
            z_out.at[pl.ds(at_row, PR)],
            z_in.at[source, step],
            sent.at[2],
            z_r.at[source],
            z_peer(step, jnp.where(f == 2, 2, c)),
        )

    chunk = c * NY + y

    def deliver(step, k, target, m):
        rows_a = pl.ds(0, PA)
        return send(
            x_out.at[k, rows_a],
            lev.at[m, chunk, z, rows_a],
            sent.at[2 + target],
            gz_r.at[m, GROUP[step]],
            z_peer(step, target),
        )

    def deliver_b(step, k, target, m):
        rows_b = pl.ds(PA, PB)
        return send(
            x_out.at[k, rows_b],
            lev.at[m, chunk, z, rows_b],
            sent.at[2 + target],
            gb_r.at[m],
            (target, at(z, lax.rem(y + step, NY), c)),
        )

    def deliveries():
        def both(pairs, first=0):
            return [deliver_b(step, *p) for step in (2, 1, 3, 0)[: NY - first] for p in pairs] + [
                deliver(step, *p) for step in DELIVER if step >= first for p in pairs
            ]

        return (
            ((f == 0) & summing, lambda: both(((1, 3, 1), (1, 2, 0), (0, 1, 0)))),
            ((f == 1) & summing, lambda: both(((1, 3, 1), (1, 2, 0)))),
            ((f == 1) & summing, lambda: both(((0, 1, 0),), 1)),
            (f == 2, lambda: both(((0, 3, 0),))),
        )

    sending = f < 3

    def states(j, half):
        with scope("st"):
            loaded(j, half)
            yc = chunk_at(j)
            side = (1 - c, c)[half]
            for i in range(CH):
                value = state(side * HALF + yc * CH + i)
                span = pl.ds(pl.multiple_of(yc * CR + i * D, D), D)
                if half == 0:
                    sib_out[span] = value.astype(jnp.bfloat16)
                else:
                    part[span] = value

    def add_sib(j):
        yc = chunk_at(j)
        with scope("sw"):
            sib_copy(j, yc).wait_recv()
        return part[rows(yc)] + sib_in[rows(yc)].astype(jnp.float32)

    def send_y(j):
        y_out[j] = add_sib(j).astype(jnp.bfloat16)
        y_copies[j].start()

    @pl.when(sending)
    def _():
        states(0, 0)

    with scope("barrier"):
        pl.semaphore_wait(barrier, 7)
    signal(step_sem.at[0], z_next)
    signal(step_sem.at[3], (to_right, to_left))

    @pl.when(sending)
    def _():
        sib_copy(0, chunk_at(0)).start()
        states(0, 1)
        states(1, 0)
        sib_copy(1, chunk_at(1)).start()
        states(1, 1)

    with scope("x1"):
        pl.semaphore_wait(step_sem.at[3], 2)

    @pl.when(sending)
    def _():
        send_y(0)

    with scope("b1"):
        pl.semaphore_wait(step_sem.at[0], 2)
    signal(step_sem.at[1], z_next)

    @pl.when(sending)
    def _():
        states(2, 0)
        sib_copy(2, chunk_at(2)).start()
        states(2, 1)
        send_y(1)
        states(3, 0)
        sib_copy(3, chunk_at(3)).start()
        states(3, 1)
        send_y(2)

    with scope("b2"):
        pl.semaphore_wait(step_sem.at[1], 2)
    signal(step_sem.at[2], z_next)

    @pl.when(sending)
    def _():
        part[rows(y)] = add_sib(3)

    @pl.when(jnp.logical_not(sending))
    def _():
        for j in range(NY):
            for half in range(2):
                loaded(j, half)

    for cp in small:
        cp.wait()
    row = lax.broadcasted_iota(jnp.int32, (D, D), 0)
    floor = jnp.full((D, D), 0, jnp.int32)
    start = 0
    for i in range(4):
        low = jnp.maximum(start - wback[0, i], 0)
        floor = jnp.where(row >= start, low, floor)
        start = start + flen[0, i]
    bias[...] = jnp.where((col <= row) & (col >= floor), 0.0, -jnp.inf)
    scale1 = 1.0 / math.sqrt(D * block_tokens)
    scale2 = 1.0 / math.sqrt(D * 2 * block_tokens)
    wrows[...] = jnp.zeros_like(wrows)
    wrows[0:HEADS] = lw[0]
    wrows[HEADS : 2 * HEADS] = jnp.where(f == 2, lw[2] * scale2, lw[1] * scale1)
    wrows[2 * HEADS : 3 * HEADS] = lw[2] * scale2
    wt[...] = jnp.transpose(wrows[...])

    with scope("att0"):
        attend(0, 1)
    with scope("b3"):
        pl.semaphore_wait(step_sem.at[2], 2)
    signal(step_sem.at[4], z_next)
    with scope("att1"):
        attend(1, 4)
    with scope("b4"):
        pl.semaphore_wait(step_sem.at[4], 2)

    @pl.when(sending)
    def _():
        with scope("yw2"):
            group(3 * CR, y_r.at[0]).wait_recv()
        total = part[rows(y)]
        for i in range(3):
            total = total + y_in[i].astype(jnp.float32)
        part[rows(y)] = total
        z_out[...] = total.astype(jnp.bfloat16)
        for i in (4, 3, 5, 2, 6, 1, 7):
            z_copy(i).start()

        @pl.when((f < 2) & jnp.logical_not(summing))
        def _():
            z_copy(0).start()

    signal(step_sem.at[5], x_next)
    with scope("att2"):
        attend(4, 8)

    with scope("b5"):
        pl.semaphore_wait(step_sem.at[5], 2)

    @pl.when((f == 2) | ((f < 2) & summing))
    def _():
        total = part[pl.ds(pl.multiple_of(y * CR + z * PR, PR), PR)]
        with scope("zw"):
            group((NZ - 1) * PR, z_r.at[slot]).wait_recv()
        for i in range(1, NZ):
            total = total + z_in[slot, i].astype(jnp.float32)

        @pl.when(f == 2)
        def _():
            x_out[0] = total.astype(jnp.bfloat16)

        @pl.when(f < 2)
        def _():
            across_sum = jnp.zeros_like(total)
            with scope("zc"):
                group(CR, z_r.at[1 - slot]).wait_recv()
            for i in range(NZ):
                across_sum = across_sum + z_in[1 - slot, i].astype(jnp.float32)
            x_out[1] = (total + across_sum).astype(jnp.bfloat16)
            x_out[0] = jnp.where(f == 0, total, across_sum).astype(jnp.bfloat16)

    for who, what in deliveries():

        @pl.when(who)
        def _():
            for cp in what():
                cp.start()

    @pl.when((f == 1) & summing)
    def _():
        lev[0, chunk, z] = x_out[0]

    def gather(n):
        def same(part, ssem, rsem, dev):
            return send(part, part, ssem, rsem, dev)

        def part_a(m, yc, step):
            return lev.at[m, c * NY + yc, lax.rem(z + NZ - step, NZ), pl.ds(0, PA)]

        def part_b(m, step):
            return lev.at[m, pl.ds(c * NY, NY), lax.rem(z + NZ - step, NZ), pl.ds(PA, PB)]

        def gy(m, i, step):
            return same(part_a(m, y, step), sent.at[6 + m], gy_r.at[m, GROUP[step]], across[i][0])

        def gzb(m, step):
            return same(part_b(m, 0), sent.at[6 + m], zb_r.at[m, GROUP[step]], z_peer(step))

        source = (opp, left, right)

        def share(part, m):
            same(part, sent.at[8 + m], gs_r.at[m], sib).start()

        def read(m, chunk_index, last=True):
            level = lev[m, chunk_index].reshape(CR, D)
            for i in range(CH):
                h = chunk_index * CH + i
                value = loc[:, cols(h)] + jnp.dot(
                    qs[m, :, cols(h)], level[i * D : (i + 1) * D], preferred_element_type=jnp.float32
                )
                if last:
                    out[:, cols(h)] = value.astype(jnp.bfloat16)
                else:
                    loc[:, cols(h)] = value

        def unless_kept(some, rest):
            if n == 2:
                some()
            else:
                kept = (f == 1) & summing
                pl.when(jnp.logical_not(kept))(some)
                if rest is not None:
                    pl.when(kept)(rest)

        def forward(m, *which):
            for g in which:
                with scope("gzw%d%d" % (m, g)):
                    wait = lambda: group(PA * len(GROUPS[g]), gz_r.at[m, g]).wait_recv()
                    if g:
                        wait()
                    else:
                        unless_kept(wait, None)
                for step in GROUPS[g]:
                    for i in range(3):
                        gy(m, i, step).start()

        def forward_b(m):
            with scope("gbw%d" % m):
                unless_kept(
                    lambda: group(NY * PB, gb_r.at[m]).wait_recv(),
                    lambda: group((NY - 1) * PB, gb_r.at[m]).wait_recv(),
                )
            for step in (4, 3, 5, 2, 6, 1, 7):
                gzb(m, step).start()
            share(part_b(m, 0), m)

        def pass_on(m, g):
            with scope("gyw%d%d" % (m, g)):
                group(3 * PA * len(GROUPS[g]), gy_r.at[m, g]).wait_recv()
            for step in GROUPS[g]:
                for yc in source:
                    share(part_a(m, yc, step), m)

        def pass_on_b(m, g):
            with scope("zbw%d%d" % (m, g)):
                group(NY * PB * len(GROUPS[g]), zb_r.at[m, g]).wait_recv()
            for step in GROUPS[g]:
                share(part_b(m, step), m)

        def shared(m):
            with scope("gsw%d" % m):
                group(HALF * D, gs_r.at[m]).wait_recv()

        for m in range(n):
            forward(m, 0, 1)
            forward_b(m)
            forward(m, 2, 3)
            share(lev.at[m, c * NY + y, pl.ds(0, NZ), pl.ds(0, PA)], m)
        m = n - 1
        own = [c * NY + yc for yc in (y, *source)]
        others = [(1 - c) * NY + yc for yc in (y, *source)]
        for k in range(n):
            pass_on(k, 0)
            pass_on(k, 1)
            pass_on_b(k, 1)
            pass_on_b(k, 2)
            pass_on(k, 2)
            pass_on_b(k, 3)
            pass_on(k, 3)
            for index in own:
                if k < m:
                    read(k, index, False)
        if n == 2:
            shared(0)
            for index in others:
                read(0, index, False)
        for index in own:
            read(m, index)
        shared(m)
        for index in others:
            read(m, index)
        for k in range(n):
            group(3 * NZ * PA + (NZ - 1) * NY * PB, sent.at[6 + k]).wait_send()
            group(HALF * D, sent.at[8 + k]).wait_send()

    @pl.when(f == 0)
    def _():
        @pl.loop(0, 2 * NY)
        def _(j):
            out[:, cols(j * CH, CH)] = loc[:, cols(j * CH, CH)].astype(jnp.bfloat16)

    @pl.when((f == 1) | (f == 2))
    def _():
        gather(1)

    @pl.when(f == 3)
    def _():
        gather(2)

    @pl.when(sending)
    def _():
        with scope("tail"):
            group(HALF * D, sent.at[0]).wait_send()
        group(3 * CR, sent.at[1]).wait_send()
        keeps = (f == 2) | summing

        @pl.when(keeps)
        def _():
            group((NZ - 1) * PR, sent.at[2]).wait_send()

        @pl.when(jnp.logical_not(keeps))
        def _():
            group(CR, sent.at[2]).wait_send()

    everywhere = NZ * PA + NY * PB
    for who, target, count in (
        ((f < 2) & summing, 2, everywhere),
        ((f < 2) & summing, 3, everywhere),
        ((f == 0) & summing, 1, everywhere),
        ((f == 1) & summing, 1, everywhere - PR),
        (f == 2, 3, everywhere),
    ):

        @pl.when(who)
        def _():
            group(count, sent.at[2 + target]).wait_send()


def body(space_count, queries, keys, values, level_weight, frame_len, window_back):
    tok, width = queries.shape
    f32, bf16 = jnp.float32, jnp.bfloat16
    dma = pltpu.SemaphoreType.DMA
    anyspec = pl.BlockSpec(memory_space=pl.ANY)
    return pl.pallas_call(
        functools.partial(kernel, tok * space_count),
        out_shape=pltpu.VMEM((tok, width), bf16),
        in_specs=[anyspec] * 6,
        out_specs=pl.BlockSpec(memory_space=pltpu.VMEM),
        scratch_shapes=[
            pltpu.SMEM((1, 4), jnp.int32),
            pltpu.SMEM((1, 4), jnp.int32),
            pltpu.VMEM(level_weight.shape, f32),
            pltpu.VMEM((tok, width), bf16),
            pltpu.VMEM((tok, width), bf16),
            pltpu.VMEM((tok, width), bf16),
            pltpu.VMEM((D, D), f32),
            pltpu.VMEM((D, D), f32),
            pltpu.VMEM((D, D), f32),
            pltpu.VMEM((tok, width), f32),
            pltpu.VMEM((2, tok, width), bf16),
            pltpu.VMEM((HALF * D, D), f32),
            pltpu.VMEM((HALF * D, D), bf16),
            pltpu.VMEM((HALF * D, D), bf16),
            pltpu.VMEM((3, CR, D), bf16),
            pltpu.VMEM((3, CR, D), bf16),
            pltpu.VMEM((CR, D), bf16),
            pltpu.VMEM((2, NZ, PR, D), bf16),
            pltpu.VMEM((2, PR, D), bf16),
            pltpu.VMEM((2, 2 * NY, NZ, PR, D), bf16),
            dma((NY, 2)),
            dma((4,)),
            pltpu.SemaphoreType.REGULAR((6,)),
            dma((10,)),
            dma((NY,)),
            dma((1,)),
            dma((2,)),
            dma((2, 4)),
            dma((2,)),
            dma((2, 4)),
            dma((2, 4)),
            dma((2,)),
        ],
        compiler_params=pltpu.CompilerParams(collective_id=0, has_side_effects=True),
    )(frame_len, window_back, level_weight, queries, keys, values)


def solution(mesh):
    return jax.shard_map(
        functools.partial(body, mesh.shape["space"]),
        mesh=mesh,
        in_specs=(
            P(("frame", "space"), None),
            P(("frame", "space"), None),
            P(("frame", "space"), None),
            P(None, None, ("frame", "space")),
            P(("frame", "space"), None),
            P(("frame", "space"), None),
        ),
        out_specs=P(("frame", "space"), None),
        check_vma=False,
    )
```

```python
import contextlib
import functools
import math

import jax
import jax.numpy as jnp
from jax import lax
from jax.experimental import pallas as pl
from jax.experimental.pallas import tpu as pltpu
from jax.sharding import PartitionSpec as P

MESH = pl.DeviceIdType.MESH
HEADS = 24
HALF = 12
D = 128
EPS = 1e-06
NY = 4
NZ = 8
CH = 3
SR = D // NZ
FIRST_Y = 0
FIRST_Z = (1, 2)
DELIVER = (0, 4, 1, 3, 5, 7, 2, 6)
GROUPS = ((0, 1, 7), (2, 6), (3, 5, 4))
GROUP = (0, 0, 1, 2, 2, 2, 1, 0)


def scope(name):
    return contextlib.nullcontext()


def kernel(
    block_tokens,
    flen_hbm,
    wback_hbm,
    lw_hbm,
    q_hbm,
    k_hbm,
    v_hbm,
    out,
    flen,
    wback,
    lw,
    q,
    k,
    v,
    bias,
    wrows,
    wt,
    loc,
    qs,
    part,
    sib_out,
    sib_in,
    y_out,
    y_in,
    z_out,
    z_in,
    x_out,
    lev,
    load_sem,
    misc_sem,
    step_sem,
    sent,
    sib_r,
    y_r,
    z_r,
    gz_r,
    gb_r,
    gy_r,
    zb_r,
    gs_r,
):
    f = lax.axis_index("frame")
    s = lax.axis_index("space")
    c = lax.rem(s, 2)
    y = lax.rem(s // 2, NY)
    z = s // (2 * NY)
    right = lax.rem(y + 1, NY)
    left = lax.rem(y + NY - 1, NY)
    opp = lax.rem(y + 2, NY)

    def at(zz, yy, cc):
        return (zz * NY + yy) * 2 + cc

    sib = (f, at(z, y, 1 - c))
    to_right = (f, at(z, right, c))
    to_left = (f, at(z, left, c))
    to_opp = (f, at(z, opp, c))
    across = ((to_opp, opp), (to_right, right), (to_left, left))
    chunk_at = (opp, right, left, y)

    def z_peer(step, ff=f):
        return (ff, at(lax.rem(z + step, NZ), y, c))

    def cols(head, count=1):
        return pl.ds(pl.multiple_of(head * D, D), count * D)

    def head_rows(yc, i):
        return pl.ds(pl.multiple_of((yc * CH + i) * D, D), D)

    def z_rows(zz):
        return pl.ds(pl.multiple_of(zz * SR, SR), SR)

    def send(src, dst, ssem, rsem, dev):
        return pltpu.make_async_remote_copy(
            src_ref=src, dst_ref=dst, send_sem=ssem, recv_sem=rsem, device_id=dev, device_id_type=MESH
        )

    def group(count, sem):
        whole = sib_in.at[pl.ds(0, count)]
        return send(whole, whole, sem, sem, sib)

    for i in range(CH):
        for half in range(2):
            for yc in chunk_at:
                span = cols((1 - c, c)[half] * HALF + yc * CH + i)
                for src, dst in ((k_hbm, k), (v_hbm, v)):
                    pltpu.make_async_copy(src.at[:, span], dst.at[:, span], load_sem.at[i, half]).start()

    def loaded(i, half):
        span = pl.ds(0, 2 * NY * D)
        pltpu.make_async_copy(k_hbm.at[:, span], k.at[:, span], load_sem.at[i, half]).wait()

    small = [
        pltpu.make_async_copy(src, dst, misc_sem.at[i])
        for i, (src, dst) in enumerate(((flen_hbm, flen), (wback_hbm, wback), (lw_hbm, lw), (q_hbm, q)))
    ]
    for cp in small:
        cp.start()

    barrier = pltpu.get_barrier_semaphore()
    z_next = (z_peer(1), z_peer(NZ - 1))
    x_next = ((lax.rem(f + 1, 4), s), (lax.rem(f + 3, 4), s))

    def signal(sem, devices):
        for dev in devices:
            pl.semaphore_signal(sem, inc=1, device_id=dev, device_id_type=MESH)

    def heard(i):
        with scope("h%d" % i):
            pl.semaphore_wait(step_sem.at[i], 2)

    signal(barrier, (sib, to_right, to_left, *z_next, *x_next))

    col = lax.broadcasted_iota(jnp.int32, (D, D), 1)

    def weight(index):
        return jnp.sum(jnp.where(col == index, wt[...], 0.0), -1, keepdims=True)

    def state(head):
        kk = k[:, cols(head)].astype(jnp.float32)
        kn = (kk * lax.rsqrt(jnp.mean(kk * kk, -1, keepdims=True) + EPS)).astype(jnp.bfloat16)
        return lax.dot_general(
            kn, v[:, cols(head)], (((0,), (0,)), ((), ())), preferred_element_type=jnp.float32
        )

    def attend(first, last):
        @pl.loop(first, last)
        def _(j):
            for i in range(CH):
                h = j * CH + i
                qq = q[:, cols(h)]
                scores = lax.dot_general(
                    qq, k[:, cols(h)], (((1,), (1,)), ((), ())), preferred_element_type=jnp.float32
                )
                scores = scores + bias[...]
                top = jnp.max(scores, -1, keepdims=True)
                p = jnp.exp((scores - top) * (1.0 / math.sqrt(D)))
                total = jnp.sum(p, -1, keepdims=True)
                mix = jnp.dot(p.astype(jnp.bfloat16), v[:, cols(h)], preferred_element_type=jnp.float32)
                loc[:, cols(h)] = mix * (weight(h) / total)
                q32 = qq.astype(jnp.float32)
                r = lax.rsqrt(jnp.mean(q32 * q32, -1, keepdims=True) + EPS)
                qs[0, :, cols(h)] = (q32 * (r * weight(HEADS + h))).astype(jnp.bfloat16)
                qs[1, :, cols(h)] = (q32 * (r * weight(2 * HEADS + h))).astype(jnp.bfloat16)

    sending = f < 3

    def states(i, half):
        with scope("st"):
            loaded(i, half)
            for yc in chunk_at:
                value = state((1 - c, c)[half] * HALF + yc * CH + i)
                if half == 0:
                    sib_out[head_rows(yc, i)] = value.astype(jnp.bfloat16)
                else:
                    part[head_rows(yc, i)] = value

    def send_sib(i):
        for yc in chunk_at:
            send(sib_out.at[head_rows(yc, i)], sib_in.at[head_rows(yc, i)], sent.at[0], sib_r.at[i], sib).start()

    def send_y(i):
        with scope("sw%d" % i):
            group(NY * D, sib_r.at[i]).wait_recv()
        for n, yc in enumerate(chunk_at):
            total = part[head_rows(yc, i)] + sib_in[head_rows(yc, i)].astype(jnp.float32)
            if n < 3:
                y_out[i, n] = total.astype(jnp.bfloat16)
                send(y_out.at[i, n], y_in.at[i, n], sent.at[1], y_r.at[i], across[n][0]).start()
            else:
                part[head_rows(yc, i)] = total

    summing = c == f
    slot = jnp.where(f == 2, 0, f)
    keeps = (f == 2) | summing

    def send_z(i):
        with scope("yw%d" % i):
            group(3 * D, y_r.at[i]).wait_recv()
        total = part[head_rows(y, i)]
        for n in range(3):
            total = total + y_in[i, n].astype(jnp.float32)
        part[head_rows(y, i)] = total
        z_out[i] = total.astype(jnp.bfloat16)

        def copy(step):
            zz = lax.rem(z + step, NZ)
            target = z_peer(step, jnp.where(f == 2, 2, c))
            return send(z_out.at[i, z_rows(zz)], z_in.at[slot, i, step], sent.at[2], z_r.at[slot, i], target)

        for step in (4, 3, 5, 2, 6, 1, 7):
            copy(step).start()

        @pl.when(jnp.logical_not(keeps))
        def _():
            copy(0).start()

    chunk = c * NY + y

    def deliver(i, step, kind, target, m):
        if i == FIRST_Y:
            dev, sem = (target, at(z, lax.rem(y + step, NY), c)), gb_r.at[m]
        else:
            dev, sem = z_peer(step, target), gz_r.at[m, FIRST_Z.index(i), GROUP[step]]
        send(x_out.at[kind, i], lev.at[m, chunk, i, z_rows(z)], sent.at[2 + target], sem, dev).start()

    def finish(i):
        @pl.when(keeps)
        def _():
            total = part[pl.ds(pl.multiple_of((y * CH + i) * D + z * SR, SR), SR)]
            with scope("zw%d" % i):
                group((NZ - 1) * SR, z_r.at[slot, i]).wait_recv()
            for step in range(1, NZ):
                total = total + z_in[slot, i, step].astype(jnp.float32)

            @pl.when(f == 2)
            def _():
                x_out[0, i] = total.astype(jnp.bfloat16)

            @pl.when(f < 2)
            def _():
                more = jnp.zeros_like(total)
                with scope("zc%d" % i):
                    group(NZ * SR, z_r.at[1 - slot, i]).wait_recv()
                for step in range(NZ):
                    more = more + z_in[1 - slot, i, step].astype(jnp.float32)
                x_out[1, i] = (total + more).astype(jnp.bfloat16)
                x_out[0, i] = jnp.where(f == 0, total, more).astype(jnp.bfloat16)

        steps = (2, 1, 3, 0) if i == FIRST_Y else DELIVER
        for who, pairs, first in (
            ((f == 0) & summing, ((1, 3, 1), (1, 2, 0), (0, 1, 0)), 0),
            ((f == 1) & summing, ((1, 3, 1), (1, 2, 0)), 0),
            ((f == 1) & summing, ((0, 1, 0),), 1),
            (f == 2, ((0, 3, 0),), 0),
        ):

            @pl.when(who)
            def _():
                for step in steps:
                    for pair in pairs:
                        if step >= first:
                            deliver(i, step, *pair)

        @pl.when((f == 1) & summing)
        def _():
            lev[0, chunk, i, z_rows(z)] = x_out[0, i]

    @pl.when(sending)
    def _():
        states(0, 0)
        states(0, 1)

    with scope("barrier"):
        pl.semaphore_wait(barrier, 7)
    signal(step_sem.at[0], z_next)
    signal(step_sem.at[3], (to_right, to_left))

    @pl.when(sending)
    def _():
        send_sib(0)
        states(1, 0)
        send_sib(1)
        states(1, 1)

    heard(0)
    signal(step_sem.at[1], z_next)
    heard(3)

    @pl.when(sending)
    def _():
        send_y(0)
        states(2, 0)
        send_sib(2)
        states(2, 1)

    heard(1)
    signal(step_sem.at[2], z_next)

    @pl.when(sending)
    def _():
        send_y(1)
        send_y(2)

    heard(2)
    signal(step_sem.at[4], z_next)

    @pl.when(jnp.logical_not(sending))
    def _():
        for i in range(CH):
            for half in range(2):
                loaded(i, half)

    for cp in small:
        cp.wait()
    row = lax.broadcasted_iota(jnp.int32, (D, D), 0)
    floor = jnp.full((D, D), 0, jnp.int32)
    start = 0
    for i in range(4):
        low = jnp.maximum(start - wback[0, i], 0)
        floor = jnp.where(row >= start, low, floor)
        start = start + flen[0, i]
    bias[...] = jnp.where((col <= row) & (col >= floor), 0.0, -jnp.inf)
    scale1 = 1.0 / math.sqrt(D * block_tokens)
    scale2 = 1.0 / math.sqrt(D * 2 * block_tokens)
    wrows[...] = jnp.zeros_like(wrows)
    wrows[0:HEADS] = lw[0]
    wrows[HEADS : 2 * HEADS] = jnp.where(f == 2, lw[2] * scale2, lw[1] * scale1)
    wrows[2 * HEADS : 3 * HEADS] = lw[2] * scale2
    wt[...] = jnp.transpose(wrows[...])

    with scope("att"):
        attend(0, 1)
    heard(4)
    for i, (first, last) in enumerate(((1, 2), (2, 3), (3, 5))):

        @pl.when(sending)
        def _():
            send_z(i)

        if i == 0:
            signal(step_sem.at[5], x_next)
        with scope("att"):
            attend(first, last)
    heard(5)
    for i, (first, last) in enumerate(((5, 6), (6, 7), (7, 8))):
        finish(i)
        with scope("att"):
            attend(first, last)

    def gather(n):
        def same(ref, ssem, rsem, dev):
            return send(ref, ref, ssem, rsem, dev)

        def gy(m, i, side, step):
            ref = lev.at[m, chunk, i, z_rows(lax.rem(z + NZ - step, NZ))]
            return same(ref, sent.at[6 + m], gy_r.at[m, FIRST_Z.index(i)], across[side][0])

        def gzb(m, step):
            ref = lev.at[m, pl.ds(c * NY, NY), FIRST_Y, z_rows(z)]
            return same(ref, sent.at[6 + m], zb_r.at[m], z_peer(step))

        def share(ref, m, i):
            same(ref, sent.at[8 + m], gs_r.at[m, i], sib).start()

        def read(m, i, half):
            for yc in (y, opp, left, right):
                index = half * NY + yc
                h = index * CH + i
                value = loc[:, cols(h)] + jnp.dot(
                    qs[m, :, cols(h)], lev[m, index, i], preferred_element_type=jnp.float32
                )
                if m == n - 1:
                    out[:, cols(h)] = value.astype(jnp.bfloat16)
                else:
                    loc[:, cols(h)] = value

        def unless_kept(count, less, sem):
            if n == 2:
                group(count, sem).wait_recv()
            else:
                kept = (f == 1) & summing

                @pl.when(kept)
                def _():
                    group(count - less, sem).wait_recv()

                @pl.when(jnp.logical_not(kept))
                def _():
                    group(count, sem).wait_recv()

        def forward(m, i, g):
            count, sem = SR * len(GROUPS[g]), gz_r.at[m, FIRST_Z.index(i), g]
            with scope("gz%d%d%d" % (m, i, g)):
                if g:
                    group(count, sem).wait_recv()
                else:
                    unless_kept(count, SR, sem)
            for step in GROUPS[g]:
                for side in range(3):
                    gy(m, i, side, step).start()
            if g == 2:
                share(lev.at[m, chunk, i], m, i)

        def forward_b(m):
            with scope("gb%d" % m):
                unless_kept(NY * SR, SR, gb_r.at[m])
            for step in (4, 3, 5, 2, 6, 1, 7):
                gzb(m, step).start()

        def pass_on(m, i):
            with scope("gy%d%d" % (m, i)):
                group(3 * D, gy_r.at[m, FIRST_Z.index(i)]).wait_recv()
            for yc in (opp, left, right):
                share(lev.at[m, c * NY + yc, i], m, i)

        def pass_on_b(m):
            with scope("zb%d" % m):
                group((NZ - 1) * NY * SR, zb_r.at[m]).wait_recv()
            share(lev.at[m, pl.ds(c * NY, NY), FIRST_Y], m, FIRST_Y)

        one, two = FIRST_Z
        if n == 1:
            forward_b(0)
            for i, g in ((one, 0), (one, 1), (two, 0), (one, 2), (two, 1), (two, 2)):
                forward(0, i, g)
        else:
            forward_b(0)
            forward(0, one, 0)
            forward(0, one, 1)
            forward_b(1)
            for m, i, g in (
                (0, one, 2),
                (1, one, 0),
                (0, two, 0),
                (1, one, 1),
                (0, two, 1),
                (1, one, 2),
                (0, two, 2),
                (1, two, 0),
                (1, two, 1),
                (1, two, 2),
            ):
                forward(m, i, g)
        for i in (FIRST_Y, one, two):
            for m in range(n):
                if i == FIRST_Y:
                    pass_on_b(m)
                else:
                    pass_on(m, i)
                read(m, i, c)
        for i in (FIRST_Y, one, two):
            for m in range(n):
                with scope("gs%d%d" % (m, i)):
                    group(NY * D, gs_r.at[m, i]).wait_recv()
                read(m, i, 1 - c)
        for m in range(n):
            group(3 * 2 * NZ * SR + (NZ - 1) * NY * SR, sent.at[6 + m]).wait_send()
            group(HALF * D, sent.at[8 + m]).wait_send()

    @pl.when(f == 0)
    def _():
        @pl.loop(0, 2 * NY)
        def _(j):
            out[:, cols(j * CH, CH)] = loc[:, cols(j * CH, CH)].astype(jnp.bfloat16)

    @pl.when((f == 1) | (f == 2))
    def _():
        gather(1)

    @pl.when(f == 3)
    def _():
        gather(2)

    @pl.when(sending)
    def _():
        with scope("tail"):
            group(HALF * D, sent.at[0]).wait_send()
        group(3 * CH * D, sent.at[1]).wait_send()

        @pl.when(keeps)
        def _():
            group(CH * (NZ - 1) * SR, sent.at[2]).wait_send()

        @pl.when(jnp.logical_not(keeps))
        def _():
            group(CH * NZ * SR, sent.at[2]).wait_send()

    everywhere = 2 * NZ * SR + NY * SR
    for who, target, count in (
        ((f < 2) & summing, 2, everywhere),
        ((f < 2) & summing, 3, everywhere),
        ((f == 0) & summing, 1, everywhere),
        ((f == 1) & summing, 1, everywhere - CH * SR),
        (f == 2, 3, everywhere),
    ):

        @pl.when(who)
        def _():
            group(count, sent.at[2 + target]).wait_send()


def body(space_count, queries, keys, values, level_weight, frame_len, window_back):
    tok, width = queries.shape
    f32, bf16 = jnp.float32, jnp.bfloat16
    dma = pltpu.SemaphoreType.DMA
    anyspec = pl.BlockSpec(memory_space=pl.ANY)
    return pl.pallas_call(
        functools.partial(kernel, tok * space_count),
        out_shape=pltpu.VMEM((tok, width), bf16),
        in_specs=[anyspec] * 6,
        out_specs=pl.BlockSpec(memory_space=pltpu.VMEM),
        scratch_shapes=[
            pltpu.SMEM((1, 4), jnp.int32),
            pltpu.SMEM((1, 4), jnp.int32),
            pltpu.VMEM(level_weight.shape, f32),
            pltpu.VMEM((tok, width), bf16),
            pltpu.VMEM((tok, width), bf16),
            pltpu.VMEM((tok, width), bf16),
            pltpu.VMEM((D, D), f32),
            pltpu.VMEM((D, D), f32),
            pltpu.VMEM((D, D), f32),
            pltpu.VMEM((tok, width), f32),
            pltpu.VMEM((2, tok, width), bf16),
            pltpu.VMEM((HALF * D, D), f32),
            pltpu.VMEM((HALF * D, D), bf16),
            pltpu.VMEM((HALF * D, D), bf16),
            pltpu.VMEM((CH, 3, D, D), bf16),
            pltpu.VMEM((CH, 3, D, D), bf16),
            pltpu.VMEM((CH, D, D), bf16),
            pltpu.VMEM((2, CH, NZ, SR, D), bf16),
            pltpu.VMEM((2, CH, SR, D), bf16),
            pltpu.VMEM((2, 2 * NY, CH, D, D), bf16),
            dma((CH, 2)),
            dma((4,)),
            pltpu.SemaphoreType.REGULAR((6,)),
            dma((10,)),
            dma((CH,)),
            dma((CH,)),
            dma((2, CH)),
            dma((2, 2, 3)),
            dma((2,)),
            dma((2, 2)),
            dma((2,)),
            dma((2, CH)),
        ],
        compiler_params=pltpu.CompilerParams(collective_id=0, has_side_effects=True),
    )(frame_len, window_back, level_weight, queries, keys, values)


def solution(mesh):
    return jax.shard_map(
        functools.partial(body, mesh.shape["space"]),
        mesh=mesh,
        in_specs=(
            P(("frame", "space"), None),
            P(("frame", "space"), None),
            P(("frame", "space"), None),
            P(None, None, ("frame", "space")),
            P(("frame", "space"), None),
            P(("frame", "space"), None),
        ),
        out_specs=P(("frame", "space"), None),
        check_vma=False,
    )
```

```python
import contextlib
import functools
import math

import jax
import jax.numpy as jnp
from jax import lax
from jax.experimental import pallas as pl
from jax.experimental.pallas import tpu as pltpu
from jax.sharding import PartitionSpec as P

MESH = pl.DeviceIdType.MESH
HEADS = 24
HALF = 12
D = 128
EPS = 1e-06
NY = 4
NZ = 8
CH = 3
SR = D // NZ
FIRST_Y = 0
FIRST_Z = (1, 2)
DELIVER = (0, 4, 1, 3, 5, 7, 2, 6)
GROUPS = ((0, 1, 7), (2, 6), (3, 5, 4))
GROUP = (0, 0, 1, 2, 2, 2, 1, 0)


def scope(name):
    return contextlib.nullcontext()


def kernel(
    block_tokens,
    flen_hbm,
    wback_hbm,
    lw_hbm,
    q_hbm,
    k_hbm,
    v_hbm,
    out,
    flen,
    wback,
    lw,
    q,
    k,
    v,
    bias,
    wrows,
    wt,
    loc,
    qs,
    part,
    sib_out,
    sib_in,
    y_out,
    y_in,
    z_out,
    z_in,
    x_out,
    lev,
    load_sem,
    misc_sem,
    step_sem,
    sent,
    sib_r,
    y_r,
    z_r,
    gz_r,
    gb_r,
    gy_r,
    zb_r,
    gs_r,
):
    f = lax.axis_index("frame")
    s = lax.axis_index("space")
    c = lax.rem(s, 2)
    y = lax.rem(s // 2, NY)
    z = s // (2 * NY)
    right = lax.rem(y + 1, NY)
    left = lax.rem(y + NY - 1, NY)
    opp = lax.rem(y + 2, NY)

    def at(zz, yy, cc):
        return (zz * NY + yy) * 2 + cc

    sib = (f, at(z, y, 1 - c))
    to_right = (f, at(z, right, c))
    to_left = (f, at(z, left, c))
    to_opp = (f, at(z, opp, c))
    across = ((to_opp, opp), (to_right, right), (to_left, left))
    chunk_at = (opp, right, left, y)

    def z_peer(step, ff=f):
        return (ff, at(lax.rem(z + step, NZ), y, c))

    def cols(head, count=1):
        return pl.ds(pl.multiple_of(head * D, D), count * D)

    def head_rows(yc, i):
        return pl.ds(pl.multiple_of((yc * CH + i) * D, D), D)

    def z_rows(zz):
        return pl.ds(pl.multiple_of(zz * SR, SR), SR)

    def send(src, dst, ssem, rsem, dev):
        return pltpu.make_async_remote_copy(
            src_ref=src, dst_ref=dst, send_sem=ssem, recv_sem=rsem, device_id=dev, device_id_type=MESH
        )

    def group(count, sem):
        whole = sib_in.at[pl.ds(0, count)]
        return send(whole, whole, sem, sem, sib)

    for i in range(CH):
        for half in range(2):
            for yc in chunk_at:
                span = cols((1 - c, c)[half] * HALF + yc * CH + i)
                for src, dst in ((k_hbm, k), (v_hbm, v)):
                    pltpu.make_async_copy(src.at[:, span], dst.at[:, span], load_sem.at[i, half]).start()

    def loaded(i, half):
        span = pl.ds(0, 2 * NY * D)
        pltpu.make_async_copy(k_hbm.at[:, span], k.at[:, span], load_sem.at[i, half]).wait()

    small = [
        pltpu.make_async_copy(src, dst, misc_sem.at[i])
        for i, (src, dst) in enumerate(((flen_hbm, flen), (wback_hbm, wback), (lw_hbm, lw), (q_hbm, q)))
    ]
    for cp in small:
        cp.start()

    barrier = pltpu.get_barrier_semaphore()
    z_next = (z_peer(1), z_peer(NZ - 1))
    z_second = (z_peer(2), z_peer(NZ - 2))
    x_next = ((lax.rem(f + 1, 4), s), (lax.rem(f + 3, 4), s))

    def signal(sem, devices):
        for dev in devices:
            pl.semaphore_signal(sem, inc=1, device_id=dev, device_id_type=MESH)

    def heard(i, count=2):
        with scope("h%d" % i):
            pl.semaphore_wait(step_sem.at[i], count)

    signal(barrier, (sib, to_right, to_left, to_opp, *z_next, *x_next, *z_second))

    col = lax.broadcasted_iota(jnp.int32, (D, D), 1)

    def weight(index):
        return jnp.sum(jnp.where(col == index, wt[...], 0.0), -1, keepdims=True)

    def state(head):
        kk = k[:, cols(head)].astype(jnp.float32)
        kn = (kk * lax.rsqrt(jnp.mean(kk * kk, -1, keepdims=True) + EPS)).astype(jnp.bfloat16)
        return lax.dot_general(
            kn, v[:, cols(head)], (((0,), (0,)), ((), ())), preferred_element_type=jnp.float32
        )

    def attend(first, last):
        @pl.loop(first, last)
        def _(j):
            for i in range(CH):
                h = j * CH + i
                qq = q[:, cols(h)]
                scores = lax.dot_general(
                    qq, k[:, cols(h)], (((1,), (1,)), ((), ())), preferred_element_type=jnp.float32
                )
                scores = scores + bias[...]
                top = jnp.max(scores, -1, keepdims=True)
                p = jnp.exp((scores - top) * (1.0 / math.sqrt(D)))
                total = jnp.sum(p, -1, keepdims=True)
                mix = jnp.dot(p.astype(jnp.bfloat16), v[:, cols(h)], preferred_element_type=jnp.float32)
                loc[:, cols(h)] = mix * (weight(h) / total)
                q32 = qq.astype(jnp.float32)
                r = lax.rsqrt(jnp.mean(q32 * q32, -1, keepdims=True) + EPS)
                qs[0, :, cols(h)] = (q32 * (r * weight(HEADS + h))).astype(jnp.bfloat16)
                qs[1, :, cols(h)] = (q32 * (r * weight(2 * HEADS + h))).astype(jnp.bfloat16)

    sending = f < 3

    def states(i, half):
        with scope("st"):
            loaded(i, half)
            for yc in chunk_at:
                value = state((1 - c, c)[half] * HALF + yc * CH + i)
                if half == 0:
                    sib_out[head_rows(yc, i)] = value.astype(jnp.bfloat16)
                else:
                    part[head_rows(yc, i)] = value

    def send_sib(i):
        for yc in chunk_at:
            send(sib_out.at[head_rows(yc, i)], sib_in.at[head_rows(yc, i)], sent.at[0], sib_r.at[i], sib).start()

    def send_y(i):
        with scope("sw%d" % i):
            group(NY * D, sib_r.at[i]).wait_recv()
        for n, yc in enumerate(chunk_at):
            total = part[head_rows(yc, i)] + sib_in[head_rows(yc, i)].astype(jnp.float32)
            if n < 3:
                y_out[i, n] = total.astype(jnp.bfloat16)
                send(y_out.at[i, n], y_in.at[i, n], sent.at[1], y_r.at[i], across[n][0]).start()
            else:
                part[head_rows(yc, i)] = total

    summing = c == f
    slot = jnp.where(f == 2, 0, f)
    keeps = (f == 2) | summing

    def send_z(i):
        with scope("yw%d" % i):
            group(3 * D, y_r.at[i]).wait_recv()
        total = part[head_rows(y, i)]
        for n in range(3):
            total = total + y_in[i, n].astype(jnp.float32)
        part[head_rows(y, i)] = total
        z_out[i] = total.astype(jnp.bfloat16)

        def copy(step):
            zz = lax.rem(z + step, NZ)
            target = z_peer(step, jnp.where(f == 2, 2, c))
            return send(z_out.at[i, z_rows(zz)], z_in.at[slot, i, step], sent.at[2], z_r.at[slot, i], target)

        for step in (4, 3, 5, 2, 6, 1, 7):
            copy(step).start()

        @pl.when(jnp.logical_not(keeps))
        def _():
            copy(0).start()

    chunk = c * NY + y

    def deliver(i, step, kind, target, m):
        if i == FIRST_Y:
            dev, sem = (target, at(z, lax.rem(y + step, NY), c)), gb_r.at[m]
        else:
            dev, sem = z_peer(step, target), gz_r.at[m, FIRST_Z.index(i), GROUP[step]]
        send(x_out.at[kind, i], lev.at[m, chunk, i, z_rows(z)], sent.at[2 + target], sem, dev).start()

    def finish(i):
        @pl.when(keeps)
        def _():
            total = part[pl.ds(pl.multiple_of((y * CH + i) * D + z * SR, SR), SR)]
            with scope("zw%d" % i):
                group((NZ - 1) * SR, z_r.at[slot, i]).wait_recv()
            for step in range(1, NZ):
                total = total + z_in[slot, i, step].astype(jnp.float32)

            @pl.when(f == 2)
            def _():
                x_out[0, i] = total.astype(jnp.bfloat16)

            @pl.when(f < 2)
            def _():
                more = jnp.zeros_like(total)
                with scope("zc%d" % i):
                    group(NZ * SR, z_r.at[1 - slot, i]).wait_recv()
                for step in range(NZ):
                    more = more + z_in[1 - slot, i, step].astype(jnp.float32)
                x_out[1, i] = (total + more).astype(jnp.bfloat16)
                x_out[0, i] = jnp.where(f == 0, total, more).astype(jnp.bfloat16)

        steps = (2, 1, 3, 0) if i == FIRST_Y else DELIVER
        for who, pairs, first in (
            ((f == 0) & summing, ((1, 3, 1), (1, 2, 0), (0, 1, 0)), 0),
            ((f == 1) & summing, ((1, 3, 1), (1, 2, 0)), 0),
            ((f == 1) & summing, ((0, 1, 0),), 1),
            (f == 2, ((0, 3, 0),), 0),
        ):

            @pl.when(who)
            def _():
                for step in steps:
                    for pair in pairs:
                        if step >= first:
                            deliver(i, step, *pair)

        @pl.when((f == 1) & summing)
        def _():
            lev[0, chunk, i, z_rows(z)] = x_out[0, i]

    @pl.when(sending)
    def _():
        states(0, 0)
        states(0, 1)

    with scope("barrier"):
        pl.semaphore_wait(barrier, 10)
    signal(step_sem.at[0], z_second)

    @pl.when(sending)
    def _():
        send_sib(0)
        states(1, 0)
        send_sib(1)
        states(2, 0)
        send_sib(2)

    @pl.when(sending)
    def _():
        send_y(0)
        states(1, 1)

    @pl.when(sending)
    def _():
        send_y(1)
        states(2, 1)

    heard(0)
    signal(step_sem.at[1], (*z_next, *z_second))

    @pl.when(sending)
    def _():
        send_y(2)

    @pl.when(jnp.logical_not(sending))
    def _():
        for i in range(CH):
            for half in range(2):
                loaded(i, half)

    for cp in small:
        cp.wait()
    row = lax.broadcasted_iota(jnp.int32, (D, D), 0)
    floor = jnp.full((D, D), 0, jnp.int32)
    start = 0
    for i in range(4):
        low = jnp.maximum(start - wback[0, i], 0)
        floor = jnp.where(row >= start, low, floor)
        start = start + flen[0, i]
    bias[...] = jnp.where((col <= row) & (col >= floor), 0.0, -jnp.inf)
    scale1 = 1.0 / math.sqrt(D * block_tokens)
    scale2 = 1.0 / math.sqrt(D * 2 * block_tokens)
    wrows[...] = jnp.zeros_like(wrows)
    wrows[0:HEADS] = lw[0]
    wrows[HEADS : 2 * HEADS] = jnp.where(f == 2, lw[2] * scale2, lw[1] * scale1)
    wrows[2 * HEADS : 3 * HEADS] = lw[2] * scale2
    wt[...] = jnp.transpose(wrows[...])

    with scope("att"):
        attend(0, 2)
    heard(1, 4)
    for i, (first, last) in enumerate(((2, 3), (3, 4), (4, 6))):

        @pl.when(sending)
        def _():
            send_z(i)

        if i == 0:
            signal(step_sem.at[2], x_next)
        with scope("att"):
            attend(first, last)
    heard(2)
    for i in range(CH):
        finish(i)
    with scope("att"):
        attend(6, 8)

    def gather(n):
        def same(ref, ssem, rsem, dev):
            return send(ref, ref, ssem, rsem, dev)

        def gy(m, i, side, step):
            ref = lev.at[m, chunk, i, z_rows(lax.rem(z + NZ - step, NZ))]
            return same(ref, sent.at[6 + m], gy_r.at[m, FIRST_Z.index(i)], across[side][0])

        def gzb(m, step):
            ref = lev.at[m, pl.ds(c * NY, NY), FIRST_Y, z_rows(z)]
            return same(ref, sent.at[6 + m], zb_r.at[m], z_peer(step))

        def share(ref, m, i):
            same(ref, sent.at[8 + m], gs_r.at[m, i], sib).start()

        def read(i, half):
            for yc in (y, opp, left, right):
                index = half * NY + yc
                h = index * CH + i
                value = loc[:, cols(h)]
                for m in range(n):
                    value = value + jnp.dot(
                        qs[m, :, cols(h)], lev[m, index, i], preferred_element_type=jnp.float32
                    )
                out[:, cols(h)] = value.astype(jnp.bfloat16)

        def read_shared(i):
            for m in range(n):
                with scope("gs%d%d" % (m, i)):
                    group(NY * D, gs_r.at[m, i]).wait_recv()
            read(i, 1 - c)

        def unless_kept(count, less, sem):
            if n == 2:
                group(count, sem).wait_recv()
            else:
                kept = (f == 1) & summing

                @pl.when(kept)
                def _():
                    group(count - less, sem).wait_recv()

                @pl.when(jnp.logical_not(kept))
                def _():
                    group(count, sem).wait_recv()

        def forward(m, i, g):
            count, sem = SR * len(GROUPS[g]), gz_r.at[m, FIRST_Z.index(i), g]
            with scope("gz%d%d%d" % (m, i, g)):
                if g:
                    group(count, sem).wait_recv()
                else:
                    unless_kept(count, SR, sem)
            for step in GROUPS[g]:
                for side in range(3):
                    gy(m, i, side, step).start()
            if g == 2:
                share(lev.at[m, chunk, i], m, i)

        def forward_b(m):
            with scope("gb%d" % m):
                unless_kept(NY * SR, SR, gb_r.at[m])
            for step in (4, 3, 5, 2, 6, 1, 7):
                gzb(m, step).start()

        def pass_on(m, i):
            with scope("gy%d%d" % (m, i)):
                group(3 * D, gy_r.at[m, FIRST_Z.index(i)]).wait_recv()
            for yc in (opp, left, right):
                share(lev.at[m, c * NY + yc, i], m, i)

        def pass_on_b(m):
            with scope("zb%d" % m):
                group((NZ - 1) * NY * SR, zb_r.at[m]).wait_recv()
            share(lev.at[m, pl.ds(c * NY, NY), FIRST_Y], m, FIRST_Y)

        one, two = FIRST_Z
        if n == 1:
            forward_b(0)
            for i, g in ((one, 0), (one, 1), (two, 0), (one, 2), (two, 1), (two, 2)):
                forward(0, i, g)
        else:
            forward_b(0)
            forward(0, one, 0)
            forward_b(1)
            for m, i, g in (
                (0, one, 1),
                (0, one, 2),
                (1, one, 0),
                (0, two, 0),
                (1, one, 1),
                (0, two, 1),
                (1, one, 2),
                (0, two, 2),
                (1, two, 0),
                (1, two, 1),
                (1, two, 2),
            ):
                forward(m, i, g)
        pass_on_b(0)
        if n == 2:
            pass_on(0, one)
            pass_on_b(1)
        read(FIRST_Y, c)
        pass_on(n - 1, one)
        read(one, c)
        if n == 2:
            pass_on(0, two)
        pass_on(n - 1, two)
        read(two, c)
        for i in (FIRST_Y, one, two):
            read_shared(i)
        for m in range(n):
            group(3 * 2 * NZ * SR + (NZ - 1) * NY * SR, sent.at[6 + m]).wait_send()
            group(HALF * D, sent.at[8 + m]).wait_send()

    @pl.when(f == 0)
    def _():
        @pl.loop(0, 2 * NY)
        def _(j):
            out[:, cols(j * CH, CH)] = loc[:, cols(j * CH, CH)].astype(jnp.bfloat16)

    @pl.when((f == 1) | (f == 2))
    def _():
        gather(1)

    @pl.when(f == 3)
    def _():
        gather(2)

    @pl.when(sending)
    def _():
        with scope("tail"):
            group(HALF * D, sent.at[0]).wait_send()
        group(3 * CH * D, sent.at[1]).wait_send()

        @pl.when(keeps)
        def _():
            group(CH * (NZ - 1) * SR, sent.at[2]).wait_send()

        @pl.when(jnp.logical_not(keeps))
        def _():
            group(CH * NZ * SR, sent.at[2]).wait_send()

    everywhere = 2 * NZ * SR + NY * SR
    for who, target, count in (
        ((f < 2) & summing, 2, everywhere),
        ((f < 2) & summing, 3, everywhere),
        ((f == 0) & summing, 1, everywhere),
        ((f == 1) & summing, 1, everywhere - CH * SR),
        (f == 2, 3, everywhere),
    ):

        @pl.when(who)
        def _():
            group(count, sent.at[2 + target]).wait_send()


def body(space_count, queries, keys, values, level_weight, frame_len, window_back):
    tok, width = queries.shape
    f32, bf16 = jnp.float32, jnp.bfloat16
    dma = pltpu.SemaphoreType.DMA
    anyspec = pl.BlockSpec(memory_space=pl.ANY)
    return pl.pallas_call(
        functools.partial(kernel, tok * space_count),
        out_shape=pltpu.VMEM((tok, width), bf16),
        in_specs=[anyspec] * 6,
        out_specs=pl.BlockSpec(memory_space=pltpu.VMEM),
        scratch_shapes=[
            pltpu.SMEM((1, 4), jnp.int32),
            pltpu.SMEM((1, 4), jnp.int32),
            pltpu.VMEM(level_weight.shape, f32),
            pltpu.VMEM((tok, width), bf16),
            pltpu.VMEM((tok, width), bf16),
            pltpu.VMEM((tok, width), bf16),
            pltpu.VMEM((D, D), f32),
            pltpu.VMEM((D, D), f32),
            pltpu.VMEM((D, D), f32),
            pltpu.VMEM((tok, width), f32),
            pltpu.VMEM((2, tok, width), bf16),
            pltpu.VMEM((HALF * D, D), f32),
            pltpu.VMEM((HALF * D, D), bf16),
            pltpu.VMEM((HALF * D, D), bf16),
            pltpu.VMEM((CH, 3, D, D), bf16),
            pltpu.VMEM((CH, 3, D, D), bf16),
            pltpu.VMEM((CH, D, D), bf16),
            pltpu.VMEM((2, CH, NZ, SR, D), bf16),
            pltpu.VMEM((2, CH, SR, D), bf16),
            pltpu.VMEM((2, 2 * NY, CH, D, D), bf16),
            dma((CH, 2)),
            dma((4,)),
            pltpu.SemaphoreType.REGULAR((3,)),
            dma((10,)),
            dma((CH,)),
            dma((CH,)),
            dma((2, CH)),
            dma((2, 2, 3)),
            dma((2,)),
            dma((2, 2)),
            dma((2,)),
            dma((2, CH)),
        ],
        compiler_params=pltpu.CompilerParams(collective_id=0, has_side_effects=True),
    )(frame_len, window_back, level_weight, queries, keys, values)


def solution(mesh):
    return jax.shard_map(
        functools.partial(body, mesh.shape["space"]),
        mesh=mesh,
        in_specs=(
            P(("frame", "space"), None),
            P(("frame", "space"), None),
            P(("frame", "space"), None),
            P(None, None, ("frame", "space")),
            P(("frame", "space"), None),
            P(("frame", "space"), None),
        ),
        out_specs=P(("frame", "space"), None),
        check_vma=False,
    )
```

```python
import contextlib
import functools
import math

import jax
import jax.numpy as jnp
from jax import lax
from jax.experimental import pallas as pl
from jax.experimental.pallas import tpu as pltpu
from jax.sharding import PartitionSpec as P

MESH = pl.DeviceIdType.MESH
HEADS = 24
HALF = 12
D = 128
EPS = 1e-06
NY = 4
NZ = 8
CH = 3
SR = D // NZ
FIRST_Y = 0
FIRST_Z = (1, 2)
DELIVER = (0, 4, 1, 3, 5, 7, 2, 6)
GROUPS = ((0, 1, 7), (2, 6), (3, 5, 4))
GROUP = (0, 0, 1, 2, 2, 2, 1, 0)


def scope(name):
    return contextlib.nullcontext()


def kernel(
    block_tokens,
    flen_hbm,
    wback_hbm,
    lw_hbm,
    q_hbm,
    k_hbm,
    v_hbm,
    out,
    flen,
    wback,
    lw,
    q,
    k,
    v,
    bias,
    wrows,
    wt,
    loc,
    qs,
    part,
    sib_out,
    sib_in,
    y_out,
    y_in,
    z_out,
    z_in,
    x_out,
    lev,
    load_sem,
    misc_sem,
    step_sem,
    sent,
    sib_r,
    y_r,
    z_r,
    gz_r,
    gb_r,
    gy_r,
    zb_r,
    gs_r,
):
    f = lax.axis_index("frame")
    s = lax.axis_index("space")
    c = lax.rem(s, 2)
    y = lax.rem(s // 2, NY)
    z = s // (2 * NY)
    right = lax.rem(y + 1, NY)
    left = lax.rem(y + NY - 1, NY)
    opp = lax.rem(y + 2, NY)

    def at(zz, yy, cc):
        return (zz * NY + yy) * 2 + cc

    sib = (f, at(z, y, 1 - c))
    to_right = (f, at(z, right, c))
    to_left = (f, at(z, left, c))
    to_opp = (f, at(z, opp, c))
    across = ((to_right, right), (to_left, left), (to_opp, opp))
    chunk_at = (right, left, opp, y)

    def z_peer(step, ff=f):
        return (ff, at(lax.rem(z + step, NZ), y, c))

    def cols(head, count=1):
        return pl.ds(pl.multiple_of(head * D, D), count * D)

    def head_rows(yc, i):
        return pl.ds(pl.multiple_of((yc * CH + i) * D, D), D)

    def z_rows(zz):
        return pl.ds(pl.multiple_of(zz * SR, SR), SR)

    def send(src, dst, ssem, rsem, dev):
        return pltpu.make_async_remote_copy(
            src_ref=src, dst_ref=dst, send_sem=ssem, recv_sem=rsem, device_id=dev, device_id_type=MESH
        )

    def group(count, sem):
        whole = sib_in.at[pl.ds(0, count)]
        return send(whole, whole, sem, sem, sib)

    for i in range(CH):
        for half in range(2):
            for yc in chunk_at:
                span = cols((1 - c, c)[half] * HALF + yc * CH + i)
                for src, dst in ((k_hbm, k), (v_hbm, v)):
                    pltpu.make_async_copy(src.at[:, span], dst.at[:, span], load_sem.at[i, half]).start()

    def loaded(i, half):
        span = pl.ds(0, 2 * NY * D)
        pltpu.make_async_copy(k_hbm.at[:, span], k.at[:, span], load_sem.at[i, half]).wait()

    small = [
        pltpu.make_async_copy(src, dst, misc_sem.at[i])
        for i, (src, dst) in enumerate(((flen_hbm, flen), (wback_hbm, wback), (lw_hbm, lw), (q_hbm, q)))
    ]
    for cp in small:
        cp.start()

    barrier = pltpu.get_barrier_semaphore()
    z_next = (z_peer(1), z_peer(NZ - 1))
    z_second = (z_peer(2), z_peer(NZ - 2))
    x_next = ((lax.rem(f + 1, 4), s), (lax.rem(f + 3, 4), s))

    def signal(sem, devices):
        for dev in devices:
            pl.semaphore_signal(sem, inc=1, device_id=dev, device_id_type=MESH)

    def heard(i, count=2):
        with scope("h%d" % i):
            pl.semaphore_wait(step_sem.at[i], count)

    signal(barrier, (sib, to_right, to_left, to_opp, *z_next, *x_next, *z_second))

    col = lax.broadcasted_iota(jnp.int32, (D, D), 1)

    def weight(index):
        return jnp.sum(jnp.where(col == index, wt[...], 0.0), -1, keepdims=True)

    def state(head):
        kk = k[:, cols(head)].astype(jnp.float32)
        kn = (kk * lax.rsqrt(jnp.mean(kk * kk, -1, keepdims=True) + EPS)).astype(jnp.bfloat16)
        return lax.dot_general(
            kn, v[:, cols(head)], (((0,), (0,)), ((), ())), preferred_element_type=jnp.float32
        )

    def attend(first, last):
        @pl.loop(first, last)
        def _(j):
            for i in range(CH):
                h = j * CH + i
                qq = q[:, cols(h)]
                scores = lax.dot_general(
                    qq, k[:, cols(h)], (((1,), (1,)), ((), ())), preferred_element_type=jnp.float32
                )
                scores = scores + bias[...]
                top = jnp.max(scores, -1, keepdims=True)
                p = jnp.exp((scores - top) * (1.0 / math.sqrt(D)))
                total = jnp.sum(p, -1, keepdims=True)
                mix = jnp.dot(p.astype(jnp.bfloat16), v[:, cols(h)], preferred_element_type=jnp.float32)
                loc[:, cols(h)] = mix * (weight(h) / total)
                q32 = qq.astype(jnp.float32)
                r = lax.rsqrt(jnp.mean(q32 * q32, -1, keepdims=True) + EPS)
                qs[0, :, cols(h)] = (q32 * (r * weight(HEADS + h))).astype(jnp.bfloat16)
                qs[1, :, cols(h)] = (q32 * (r * weight(2 * HEADS + h))).astype(jnp.bfloat16)

    sending = f < 3

    def states(i, half):
        with scope("st"):
            loaded(i, half)
            for yc in chunk_at:
                value = state((1 - c, c)[half] * HALF + yc * CH + i)
                if half == 0:
                    sib_out[head_rows(yc, i)] = value.astype(jnp.bfloat16)
                else:
                    part[head_rows(yc, i)] = value

    def send_sib(i):
        for yc in chunk_at:
            send(sib_out.at[head_rows(yc, i)], sib_in.at[head_rows(yc, i)], sent.at[0], sib_r.at[i], sib).start()

    def send_y(i):
        with scope("sw%d" % i):
            group(NY * D, sib_r.at[i]).wait_recv()
        for n, yc in enumerate(chunk_at):
            total = part[head_rows(yc, i)] + sib_in[head_rows(yc, i)].astype(jnp.float32)
            if n < 3:
                y_out[i, n] = total.astype(jnp.bfloat16)
                send(y_out.at[i, n], y_in.at[i, n], sent.at[1], y_r.at[i], across[n][0]).start()
            else:
                part[head_rows(yc, i)] = total

    summing = c == f
    slot = jnp.where(f == 2, 0, f)
    keeps = (f == 2) | summing

    def send_z(i):
        with scope("yw%d" % i):
            group(3 * D, y_r.at[i]).wait_recv()
        total = part[head_rows(y, i)]
        for n in range(3):
            total = total + y_in[i, n].astype(jnp.float32)
        part[head_rows(y, i)] = total
        z_out[i] = total.astype(jnp.bfloat16)

        def copy(step):
            zz = lax.rem(z + step, NZ)
            target = z_peer(step, jnp.where(f == 2, 2, c))
            return send(z_out.at[i, z_rows(zz)], z_in.at[slot, i, step], sent.at[2], z_r.at[slot, i], target)

        for step in (4, 3, 5, 2, 6, 1, 7):
            copy(step).start()

        @pl.when(jnp.logical_not(keeps))
        def _():
            copy(0).start()

    chunk = c * NY + y

    def deliver(i, step, kind, target, m):
        if i == FIRST_Y:
            dev, sem = (target, at(z, lax.rem(y + step, NY), c)), gb_r.at[m]
        else:
            dev, sem = z_peer(step, target), gz_r.at[m, FIRST_Z.index(i), GROUP[step]]
        send(x_out.at[kind, i], lev.at[m, chunk, i, z_rows(z)], sent.at[2 + target], sem, dev).start()

    def finish(i):
        @pl.when(keeps)
        def _():
            total = part[pl.ds(pl.multiple_of((y * CH + i) * D + z * SR, SR), SR)]
            with scope("zw%d" % i):
                group((NZ - 1) * SR, z_r.at[slot, i]).wait_recv()
            for step in range(1, NZ):
                total = total + z_in[slot, i, step].astype(jnp.float32)

            @pl.when(f == 2)
            def _():
                x_out[0, i] = total.astype(jnp.bfloat16)

            @pl.when(f < 2)
            def _():
                more = jnp.zeros_like(total)
                with scope("zc%d" % i):
                    group(NZ * SR, z_r.at[1 - slot, i]).wait_recv()
                for step in range(NZ):
                    more = more + z_in[1 - slot, i, step].astype(jnp.float32)
                x_out[1, i] = (total + more).astype(jnp.bfloat16)
                x_out[0, i] = jnp.where(f == 0, total, more).astype(jnp.bfloat16)

        steps = (2, 1, 3, 0) if i == FIRST_Y else DELIVER
        for who, pairs, first in (
            ((f == 0) & summing, ((1, 3, 1), (1, 2, 0), (0, 1, 0)), 0),
            ((f == 1) & summing, ((1, 3, 1), (1, 2, 0)), 0),
            ((f == 1) & summing, ((0, 1, 0),), 1),
            (f == 2, ((0, 3, 0),), 0),
        ):

            @pl.when(who)
            def _():
                for step in steps:
                    for pair in pairs:
                        if step >= first:
                            deliver(i, step, *pair)

        @pl.when((f == 1) & summing)
        def _():
            lev[0, chunk, i, z_rows(z)] = x_out[0, i]

    @pl.when(sending)
    def _():
        states(0, 0)
        states(0, 1)

    with scope("barrier"):
        pl.semaphore_wait(barrier, 10)
    signal(step_sem.at[0], z_second)

    @pl.when(sending)
    def _():
        send_sib(0)
        states(1, 0)
        send_sib(1)
        states(2, 0)
        send_sib(2)

    @pl.when(sending)
    def _():
        send_y(0)
        states(1, 1)

    @pl.when(sending)
    def _():
        send_y(1)
        states(2, 1)

    heard(0)
    signal(step_sem.at[1], (*z_next, *z_second))

    @pl.when(sending)
    def _():
        send_y(2)

    @pl.when(jnp.logical_not(sending))
    def _():
        for i in range(CH):
            for half in range(2):
                loaded(i, half)

    for cp in small:
        cp.wait()
    row = lax.broadcasted_iota(jnp.int32, (D, D), 0)
    floor = jnp.full((D, D), 0, jnp.int32)
    start = 0
    for i in range(4):
        low = jnp.maximum(start - wback[0, i], 0)
        floor = jnp.where(row >= start, low, floor)
        start = start + flen[0, i]
    bias[...] = jnp.where((col <= row) & (col >= floor), 0.0, -jnp.inf)
    scale1 = 1.0 / math.sqrt(D * block_tokens)
    scale2 = 1.0 / math.sqrt(D * 2 * block_tokens)
    wrows[...] = jnp.zeros_like(wrows)
    wrows[0:HEADS] = lw[0]
    wrows[HEADS : 2 * HEADS] = jnp.where(f == 2, lw[2] * scale2, lw[1] * scale1)
    wrows[2 * HEADS : 3 * HEADS] = lw[2] * scale2
    wt[...] = jnp.transpose(wrows[...])

    with scope("att"):
        attend(0, 2)
    heard(1, 4)
    for i, (first, last) in enumerate(((2, 3), (3, 4), (4, 6))):

        @pl.when(sending)
        def _():
            send_z(i)

        if i == 0:
            signal(step_sem.at[2], x_next)
        with scope("att"):
            attend(first, last)
    heard(2)
    for i in range(CH):
        finish(i)
    with scope("att"):
        attend(6, 8)

    def gather(n):
        def same(ref, ssem, rsem, dev):
            return send(ref, ref, ssem, rsem, dev)

        def gy(m, i, side, step):
            ref = lev.at[m, chunk, i, z_rows(lax.rem(z + NZ - step, NZ))]
            return same(ref, sent.at[6 + m], gy_r.at[m, FIRST_Z.index(i)], across[side][0])

        def gzb(m, step):
            ref = lev.at[m, pl.ds(c * NY, NY), FIRST_Y, z_rows(z)]
            return same(ref, sent.at[6 + m], zb_r.at[m], z_peer(step))

        def share(ref, m, i):
            same(ref, sent.at[8 + m], gs_r.at[m, i], sib).start()

        def read(i, half):
            for yc in (y, opp, left, right):
                index = half * NY + yc
                h = index * CH + i
                value = loc[:, cols(h)]
                for m in range(n):
                    value = value + jnp.dot(
                        qs[m, :, cols(h)], lev[m, index, i], preferred_element_type=jnp.float32
                    )
                out[:, cols(h)] = value.astype(jnp.bfloat16)

        def read_shared(i):
            for m in range(n):
                with scope("gs%d%d" % (m, i)):
                    group(NY * D, gs_r.at[m, i]).wait_recv()
            read(i, 1 - c)

        def unless_kept(count, less, sem):
            if n == 2:
                group(count, sem).wait_recv()
            else:
                kept = (f == 1) & summing

                @pl.when(kept)
                def _():
                    group(count - less, sem).wait_recv()

                @pl.when(jnp.logical_not(kept))
                def _():
                    group(count, sem).wait_recv()

        def forward(m, i, g):
            count, sem = SR * len(GROUPS[g]), gz_r.at[m, FIRST_Z.index(i), g]
            with scope("gz%d%d%d" % (m, i, g)):
                if g:
                    group(count, sem).wait_recv()
                else:
                    unless_kept(count, SR, sem)
            for step in GROUPS[g]:
                for side in range(3):
                    gy(m, i, side, step).start()
            if g == 2:
                share(lev.at[m, chunk, i], m, i)

        def forward_b(m):
            with scope("gb%d" % m):
                unless_kept(NY * SR, SR, gb_r.at[m])
            for step in (4, 3, 5, 2, 6, 1, 7):
                gzb(m, step).start()

        def pass_on(m, i):
            with scope("gy%d%d" % (m, i)):
                group(3 * D, gy_r.at[m, FIRST_Z.index(i)]).wait_recv()
            for yc in (opp, left, right):
                share(lev.at[m, c * NY + yc, i], m, i)

        def pass_on_b(m):
            with scope("zb%d" % m):
                group((NZ - 1) * NY * SR, zb_r.at[m]).wait_recv()
            share(lev.at[m, pl.ds(c * NY, NY), FIRST_Y], m, FIRST_Y)

        one, two = FIRST_Z
        if n == 1:
            forward_b(0)
            for i, g in ((one, 0), (one, 1), (two, 0), (one, 2), (two, 1), (two, 2)):
                forward(0, i, g)
        else:
            forward_b(0)
            forward(0, one, 0)
            forward_b(1)
            for m, i, g in (
                (0, one, 1),
                (0, one, 2),
                (1, one, 0),
                (0, two, 0),
                (1, one, 1),
                (0, two, 1),
                (1, one, 2),
                (0, two, 2),
                (1, two, 0),
                (1, two, 1),
                (1, two, 2),
            ):
                forward(m, i, g)
        pass_on_b(0)
        if n == 2:
            pass_on(0, one)
            pass_on_b(1)
        read(FIRST_Y, c)
        pass_on(n - 1, one)
        read(one, c)
        if n == 2:
            pass_on(0, two)
        pass_on(n - 1, two)
        read(two, c)
        for i in (FIRST_Y, one, two):
            read_shared(i)
        for m in range(n):
            group(3 * 2 * NZ * SR + (NZ - 1) * NY * SR, sent.at[6 + m]).wait_send()
            group(HALF * D, sent.at[8 + m]).wait_send()

    @pl.when(f == 0)
    def _():
        @pl.loop(0, 2 * NY)
        def _(j):
            out[:, cols(j * CH, CH)] = loc[:, cols(j * CH, CH)].astype(jnp.bfloat16)

    @pl.when((f == 1) | (f == 2))
    def _():
        gather(1)

    @pl.when(f == 3)
    def _():
        gather(2)

    @pl.when(sending)
    def _():
        with scope("tail"):
            group(HALF * D, sent.at[0]).wait_send()
        group(3 * CH * D, sent.at[1]).wait_send()

        @pl.when(keeps)
        def _():
            group(CH * (NZ - 1) * SR, sent.at[2]).wait_send()

        @pl.when(jnp.logical_not(keeps))
        def _():
            group(CH * NZ * SR, sent.at[2]).wait_send()

    everywhere = 2 * NZ * SR + NY * SR
    for who, target, count in (
        ((f < 2) & summing, 2, everywhere),
        ((f < 2) & summing, 3, everywhere),
        ((f == 0) & summing, 1, everywhere),
        ((f == 1) & summing, 1, everywhere - CH * SR),
        (f == 2, 3, everywhere),
    ):

        @pl.when(who)
        def _():
            group(count, sent.at[2 + target]).wait_send()


def body(space_count, queries, keys, values, level_weight, frame_len, window_back):
    tok, width = queries.shape
    f32, bf16 = jnp.float32, jnp.bfloat16
    dma = pltpu.SemaphoreType.DMA
    anyspec = pl.BlockSpec(memory_space=pl.ANY)
    return pl.pallas_call(
        functools.partial(kernel, tok * space_count),
        out_shape=pltpu.VMEM((tok, width), bf16),
        in_specs=[anyspec] * 6,
        out_specs=pl.BlockSpec(memory_space=pltpu.VMEM),
        scratch_shapes=[
            pltpu.SMEM((1, 4), jnp.int32),
            pltpu.SMEM((1, 4), jnp.int32),
            pltpu.VMEM(level_weight.shape, f32),
            pltpu.VMEM((tok, width), bf16),
            pltpu.VMEM((tok, width), bf16),
            pltpu.VMEM((tok, width), bf16),
            pltpu.VMEM((D, D), f32),
            pltpu.VMEM((D, D), f32),
            pltpu.VMEM((D, D), f32),
            pltpu.VMEM((tok, width), f32),
            pltpu.VMEM((2, tok, width), bf16),
            pltpu.VMEM((HALF * D, D), f32),
            pltpu.VMEM((HALF * D, D), bf16),
            pltpu.VMEM((HALF * D, D), bf16),
            pltpu.VMEM((CH, 3, D, D), bf16),
            pltpu.VMEM((CH, 3, D, D), bf16),
            pltpu.VMEM((CH, D, D), bf16),
            pltpu.VMEM((2, CH, NZ, SR, D), bf16),
            pltpu.VMEM((2, CH, SR, D), bf16),
            pltpu.VMEM((2, 2 * NY, CH, D, D), bf16),
            dma((CH, 2)),
            dma((4,)),
            pltpu.SemaphoreType.REGULAR((3,)),
            dma((10,)),
            dma((CH,)),
            dma((CH,)),
            dma((2, CH)),
            dma((2, 2, 3)),
            dma((2,)),
            dma((2, 2)),
            dma((2,)),
            dma((2, CH)),
        ],
        compiler_params=pltpu.CompilerParams(collective_id=0, has_side_effects=True),
    )(frame_len, window_back, level_weight, queries, keys, values)


def solution(mesh):
    return jax.shard_map(
        functools.partial(body, mesh.shape["space"]),
        mesh=mesh,
        in_specs=(
            P(("frame", "space"), None),
            P(("frame", "space"), None),
            P(("frame", "space"), None),
            P(None, None, ("frame", "space")),
            P(("frame", "space"), None),
            P(("frame", "space"), None),
        ),
        out_specs=P(("frame", "space"), None),
        check_vma=False,
    )
```

```python
import contextlib
import functools
import math

import jax
import jax.numpy as jnp
from jax import lax
from jax.experimental import pallas as pl
from jax.experimental.pallas import tpu as pltpu
from jax.sharding import PartitionSpec as P

MESH = pl.DeviceIdType.MESH
HEADS = 24
HALF = 12
D = 128
EPS = 1e-06
NY = 4
NZ = 8
CH = 3
SR = D // NZ
FIRST_Y = 0
FIRST_Z = (1, 2)
DELIVER = (0, 4, 1, 3, 5, 7, 2, 6)
GROUPS = ((0, 1, 7), (2, 6), (3, 5, 4))
GROUP = (0, 0, 1, 2, 2, 2, 1, 0)


def scope(name):
    return contextlib.nullcontext()


def kernel(
    block_tokens,
    flen_hbm,
    wback_hbm,
    lw_hbm,
    q_hbm,
    k_hbm,
    v_hbm,
    out,
    flen,
    wback,
    lw,
    q,
    k,
    v,
    bias,
    wrows,
    wt,
    loc,
    qs,
    part,
    sib_out,
    sib_in,
    y_out,
    y_in,
    z_out,
    z_in,
    x_out,
    lev,
    load_sem,
    misc_sem,
    step_sem,
    sent,
    sib_r,
    y_r,
    z_r,
    gz_r,
    gb_r,
    gy_r,
    zb_r,
    gs_r,
):
    f = lax.axis_index("frame")
    s = lax.axis_index("space")
    c = lax.rem(s, 2)
    y = lax.rem(s // 2, NY)
    z = s // (2 * NY)
    right = lax.rem(y + 1, NY)
    left = lax.rem(y + NY - 1, NY)
    opp = lax.rem(y + 2, NY)

    def at(zz, yy, cc):
        return (zz * NY + yy) * 2 + cc

    sib = (f, at(z, y, 1 - c))
    to_right = (f, at(z, right, c))
    to_left = (f, at(z, left, c))
    to_opp = (f, at(z, opp, c))
    across = ((to_right, right), (to_left, left), (to_opp, opp))
    chunk_at = (right, left, opp, y)

    def z_peer(step, ff=f):
        return (ff, at(lax.rem(z + step, NZ), y, c))

    def cols(head, count=1):
        return pl.ds(pl.multiple_of(head * D, D), count * D)

    def head_rows(yc, i):
        return pl.ds(pl.multiple_of((yc * CH + i) * D, D), D)

    def z_rows(zz):
        return pl.ds(pl.multiple_of(zz * SR, SR), SR)

    def send(src, dst, ssem, rsem, dev):
        return pltpu.make_async_remote_copy(
            src_ref=src, dst_ref=dst, send_sem=ssem, recv_sem=rsem, device_id=dev, device_id_type=MESH
        )

    def group(count, sem):
        whole = sib_in.at[pl.ds(0, count)]
        return send(whole, whole, sem, sem, sib)

    for i in range(CH):
        for half in range(2):
            for yc in chunk_at:
                span = cols((1 - c, c)[half] * HALF + yc * CH + i)
                for src, dst in ((k_hbm, k), (v_hbm, v)):
                    pltpu.make_async_copy(src.at[:, span], dst.at[:, span], load_sem.at[i, half]).start()

    def loaded(i, half):
        span = pl.ds(0, 2 * NY * D)
        pltpu.make_async_copy(k_hbm.at[:, span], k.at[:, span], load_sem.at[i, half]).wait()

    small = [
        pltpu.make_async_copy(src, dst, misc_sem.at[i])
        for i, (src, dst) in enumerate(((flen_hbm, flen), (wback_hbm, wback), (lw_hbm, lw), (q_hbm, q)))
    ]
    for cp in small:
        cp.start()

    barrier = pltpu.get_barrier_semaphore()
    z_next = (z_peer(1), z_peer(NZ - 1))
    z_second = (z_peer(2), z_peer(NZ - 2))
    x_next = ((lax.rem(f + 1, 4), s), (lax.rem(f + 3, 4), s))

    def signal(sem, devices):
        for dev in devices:
            pl.semaphore_signal(sem, inc=1, device_id=dev, device_id_type=MESH)

    def heard(i, count=2):
        with scope("h%d" % i):
            pl.semaphore_wait(step_sem.at[i], count)

    signal(barrier, (sib, to_right, to_left, to_opp, *z_next, *x_next, *z_second))

    col = lax.broadcasted_iota(jnp.int32, (D, D), 1)

    def weight(index):
        return jnp.sum(jnp.where(col == index, wt[...], 0.0), -1, keepdims=True)

    def state(head):
        kk = k[:, cols(head)].astype(jnp.float32)
        kn = (kk * lax.rsqrt(jnp.mean(kk * kk, -1, keepdims=True) + EPS)).astype(jnp.bfloat16)
        return lax.dot_general(
            kn, v[:, cols(head)], (((0,), (0,)), ((), ())), preferred_element_type=jnp.float32
        )

    def attend(first, last):
        @pl.loop(first, last)
        def _(j):
            for i in range(CH):
                h = j * CH + i
                qq = q[:, cols(h)]
                scores = lax.dot_general(
                    qq, k[:, cols(h)], (((1,), (1,)), ((), ())), preferred_element_type=jnp.float32
                )
                scores = scores + bias[...]
                top = jnp.max(scores, -1, keepdims=True)
                p = jnp.exp((scores - top) * (1.0 / math.sqrt(D)))
                total = jnp.sum(p, -1, keepdims=True)
                mix = jnp.dot(p.astype(jnp.bfloat16), v[:, cols(h)], preferred_element_type=jnp.float32)
                loc[:, cols(h)] = mix * (weight(h) / total)
                q32 = qq.astype(jnp.float32)
                r = lax.rsqrt(jnp.mean(q32 * q32, -1, keepdims=True) + EPS)
                qs[0, :, cols(h)] = (q32 * (r * weight(HEADS + h))).astype(jnp.bfloat16)
                qs[1, :, cols(h)] = (q32 * (r * weight(2 * HEADS + h))).astype(jnp.bfloat16)

    sending = f < 3

    def states(i, half):
        with scope("st"):
            loaded(i, half)
            for yc in chunk_at:
                value = state((1 - c, c)[half] * HALF + yc * CH + i)
                if half == 0:
                    sib_out[head_rows(yc, i)] = value.astype(jnp.bfloat16)
                else:
                    part[head_rows(yc, i)] = value

    def send_sib(i):
        for yc in chunk_at:
            send(sib_out.at[head_rows(yc, i)], sib_in.at[head_rows(yc, i)], sent.at[0], sib_r.at[i], sib).start()

    def send_y(i):
        with scope("sw%d" % i):
            group(NY * D, sib_r.at[i]).wait_recv()
        for n, yc in enumerate(chunk_at):
            total = part[head_rows(yc, i)] + sib_in[head_rows(yc, i)].astype(jnp.float32)
            if n < 3:
                y_out[i, n] = total.astype(jnp.bfloat16)
                send(y_out.at[i, n], y_in.at[i, n], sent.at[1], y_r.at[i], across[n][0]).start()
            else:
                part[head_rows(yc, i)] = total

    summing = c == f
    slot = jnp.where(f == 2, 0, f)
    keeps = (f == 2) | summing

    def send_z(i):
        with scope("yw%d" % i):
            group(3 * D, y_r.at[i]).wait_recv()
        total = part[head_rows(y, i)]
        for n in range(3):
            total = total + y_in[i, n].astype(jnp.float32)
        part[head_rows(y, i)] = total
        z_out[i] = total.astype(jnp.bfloat16)

        def copy(step):
            zz = lax.rem(z + step, NZ)
            target = z_peer(step, jnp.where(f == 2, 2, c))
            return send(z_out.at[i, z_rows(zz)], z_in.at[slot, i, step], sent.at[2], z_r.at[slot, i], target)

        for step in (4, 3, 5, 2, 6, 1, 7):
            copy(step).start()

        @pl.when(jnp.logical_not(keeps))
        def _():
            copy(0).start()

    chunk = c * NY + y

    def deliver(i, step, kind, target, m):
        if i == FIRST_Y:
            dev, sem = (target, at(z, lax.rem(y + step, NY), c)), gb_r.at[m]
        else:
            dev, sem = z_peer(step, target), gz_r.at[m, FIRST_Z.index(i), GROUP[step]]
        send(x_out.at[kind, i], lev.at[m, chunk, i, z_rows(z)], sent.at[2], sem, dev).start()

    def finish(i):
        @pl.when(keeps)
        def _():
            total = part[pl.ds(pl.multiple_of((y * CH + i) * D + z * SR, SR), SR)]
            with scope("zw%d" % i):
                group((NZ - 1) * SR, z_r.at[slot, i]).wait_recv()
            for step in range(1, NZ):
                total = total + z_in[slot, i, step].astype(jnp.float32)

            @pl.when(f == 2)
            def _():
                x_out[0, i] = total.astype(jnp.bfloat16)

            @pl.when(f < 2)
            def _():
                more = jnp.zeros_like(total)
                with scope("zc%d" % i):
                    group(NZ * SR, z_r.at[1 - slot, i]).wait_recv()
                for step in range(NZ):
                    more = more + z_in[1 - slot, i, step].astype(jnp.float32)
                x_out[1, i] = (total + more).astype(jnp.bfloat16)
                x_out[0, i] = jnp.where(f == 0, total, more).astype(jnp.bfloat16)

        steps = (2, 1, 3, 0) if i == FIRST_Y else DELIVER
        for who, pairs, first in (
            ((f == 0) & summing, ((1, 3, 1), (1, 2, 0), (0, 1, 0)), 0),
            ((f == 1) & summing, ((1, 3, 1), (1, 2, 0)), 0),
            ((f == 1) & summing, ((0, 1, 0),), 1),
            (f == 2, ((0, 3, 0),), 0),
        ):

            @pl.when(who)
            def _():
                for step in steps:
                    for pair in pairs:
                        if step >= first:
                            deliver(i, step, *pair)

        @pl.when((f == 1) & summing)
        def _():
            lev[0, chunk, i, z_rows(z)] = x_out[0, i]

    @pl.when(sending)
    def _():
        states(0, 0)
        states(0, 1)

    with scope("barrier"):
        pl.semaphore_wait(barrier, 10)
    signal(step_sem.at[0], z_second)

    @pl.when(sending)
    def _():
        send_sib(0)
        states(1, 0)
        send_sib(1)
        states(2, 0)
        send_sib(2)

    @pl.when(sending)
    def _():
        send_y(0)
        states(1, 1)

    @pl.when(sending)
    def _():
        send_y(1)
        states(2, 1)

    heard(0)
    signal(step_sem.at[1], (*z_next, *z_second))

    @pl.when(sending)
    def _():
        send_y(2)

    @pl.when(jnp.logical_not(sending))
    def _():
        for i in range(CH):
            for half in range(2):
                loaded(i, half)

    for cp in small:
        cp.wait()
    row = lax.broadcasted_iota(jnp.int32, (D, D), 0)
    floor = jnp.full((D, D), 0, jnp.int32)
    start = 0
    for i in range(4):
        low = jnp.maximum(start - wback[0, i], 0)
        floor = jnp.where(row >= start, low, floor)
        start = start + flen[0, i]
    bias[...] = jnp.where((col <= row) & (col >= floor), 0.0, -jnp.inf)
    scale1 = 1.0 / math.sqrt(D * block_tokens)
    scale2 = 1.0 / math.sqrt(D * 2 * block_tokens)
    wrows[...] = jnp.zeros_like(wrows)
    wrows[0:HEADS] = lw[0]
    wrows[HEADS : 2 * HEADS] = jnp.where(f == 2, lw[2] * scale2, lw[1] * scale1)
    wrows[2 * HEADS : 3 * HEADS] = lw[2] * scale2
    wt[...] = jnp.transpose(wrows[...])

    with scope("att"):
        attend(0, 2)
    heard(1, 4)
    for i, (first, last) in enumerate(((2, 3), (3, 4), (4, 5))):

        @pl.when(sending)
        def _():
            send_z(i)

        if i == 0:
            signal(step_sem.at[2], x_next)
        with scope("att"):
            attend(first, last)
    heard(2)
    for i in range(CH):
        finish(i)
    with scope("att"):
        attend(5, 8)

    def gather(n):
        def same(ref, ssem, rsem, dev):
            return send(ref, ref, ssem, rsem, dev)

        def gy(m, i, side, step):
            ref = lev.at[m, chunk, i, z_rows(lax.rem(z + NZ - step, NZ))]
            return same(ref, sent.at[3 + m], gy_r.at[m, FIRST_Z.index(i)], across[side][0])

        def gzb(m, step):
            ref = lev.at[m, pl.ds(c * NY, NY), FIRST_Y, z_rows(z)]
            return same(ref, sent.at[3 + m], zb_r.at[m], z_peer(step))

        def share(ref, m, i):
            same(ref, sent.at[5 + m], gs_r.at[m, i], sib).start()

        def read(i, half):
            for yc in (y, opp, left, right):
                index = half * NY + yc
                h = index * CH + i
                value = loc[:, cols(h)]
                for m in range(n):
                    value = value + jnp.dot(
                        qs[m, :, cols(h)], lev[m, index, i], preferred_element_type=jnp.float32
                    )
                out[:, cols(h)] = value.astype(jnp.bfloat16)

        def read_shared(i):
            for m in range(n):
                with scope("gs%d%d" % (m, i)):
                    group(NY * D, gs_r.at[m, i]).wait_recv()
            read(i, 1 - c)

        def unless_kept(count, less, sem):
            if n == 2:
                group(count, sem).wait_recv()
            else:
                kept = (f == 1) & summing

                @pl.when(kept)
                def _():
                    group(count - less, sem).wait_recv()

                @pl.when(jnp.logical_not(kept))
                def _():
                    group(count, sem).wait_recv()

        def forward(m, i, g):
            count, sem = SR * len(GROUPS[g]), gz_r.at[m, FIRST_Z.index(i), g]
            with scope("gz%d%d%d" % (m, i, g)):
                if g:
                    group(count, sem).wait_recv()
                else:
                    unless_kept(count, SR, sem)
            for step in GROUPS[g]:
                for side in range(3):
                    gy(m, i, side, step).start()
            if g == 2:
                share(lev.at[m, chunk, i], m, i)

        def forward_b(m):
            with scope("gb%d" % m):
                unless_kept(NY * SR, SR, gb_r.at[m])
            for step in (4, 3, 5, 2, 6, 1, 7):
                gzb(m, step).start()

        def pass_on(m, i):
            with scope("gy%d%d" % (m, i)):
                group(3 * D, gy_r.at[m, FIRST_Z.index(i)]).wait_recv()
            for yc in (opp, left, right):
                share(lev.at[m, c * NY + yc, i], m, i)

        def pass_on_b(m):
            with scope("zb%d" % m):
                group((NZ - 1) * NY * SR, zb_r.at[m]).wait_recv()
            share(lev.at[m, pl.ds(c * NY, NY), FIRST_Y], m, FIRST_Y)

        one, two = FIRST_Z
        if n == 1:
            forward_b(0)
            for i, g in ((one, 0), (one, 1), (two, 0), (one, 2), (two, 1), (two, 2)):
                forward(0, i, g)
        else:
            forward_b(0)
            forward(0, one, 0)
            forward_b(1)
            for m, i, g in (
                (0, one, 1),
                (0, one, 2),
                (1, one, 0),
                (0, two, 0),
                (1, one, 1),
                (0, two, 1),
                (1, one, 2),
                (0, two, 2),
                (1, two, 0),
                (1, two, 1),
                (1, two, 2),
            ):
                forward(m, i, g)
        pass_on_b(0)
        if n == 2:
            pass_on(0, one)
            pass_on_b(1)
        read(FIRST_Y, c)
        pass_on(n - 1, one)
        read(one, c)
        if n == 2:
            pass_on(0, two)
        pass_on(n - 1, two)
        read(two, c)
        for i in (FIRST_Y, one, two):
            read_shared(i)
        for m in range(n):
            group(3 * 2 * NZ * SR + (NZ - 1) * NY * SR, sent.at[3 + m]).wait_send()
            group(HALF * D, sent.at[5 + m]).wait_send()

    @pl.when(f == 0)
    def _():
        @pl.loop(0, 2 * NY)
        def _(j):
            out[:, cols(j * CH, CH)] = loc[:, cols(j * CH, CH)].astype(jnp.bfloat16)

    @pl.when((f == 1) | (f == 2))
    def _():
        gather(1)

    @pl.when(f == 3)
    def _():
        gather(2)

    @pl.when(sending)
    def _():
        with scope("tail"):
            group(HALF * D, sent.at[0]).wait_send()
        group(3 * CH * D, sent.at[1]).wait_send()

    own, everywhere = CH * (NZ - 1) * SR, 2 * NZ * SR + NY * SR
    for who, count in (
        ((f < 3) & jnp.logical_not(keeps), CH * NZ * SR),
        ((f == 0) & summing, own + 3 * everywhere),
        ((f == 1) & summing, own + 3 * everywhere - CH * SR),
        (f == 2, own + everywhere),
    ):

        @pl.when(who)
        def _():
            group(count, sent.at[2]).wait_send()


def body(space_count, queries, keys, values, level_weight, frame_len, window_back):
    tok, width = queries.shape
    f32, bf16 = jnp.float32, jnp.bfloat16
    dma = pltpu.SemaphoreType.DMA
    anyspec = pl.BlockSpec(memory_space=pl.ANY)
    return pl.pallas_call(
        functools.partial(kernel, tok * space_count),
        out_shape=pltpu.VMEM((tok, width), bf16),
        in_specs=[anyspec] * 6,
        out_specs=pl.BlockSpec(memory_space=pltpu.VMEM),
        scratch_shapes=[
            pltpu.SMEM((1, 4), jnp.int32),
            pltpu.SMEM((1, 4), jnp.int32),
            pltpu.VMEM(level_weight.shape, f32),
            pltpu.VMEM((tok, width), bf16),
            pltpu.VMEM((tok, width), bf16),
            pltpu.VMEM((tok, width), bf16),
            pltpu.VMEM((D, D), f32),
            pltpu.VMEM((D, D), f32),
            pltpu.VMEM((D, D), f32),
            pltpu.VMEM((tok, width), f32),
            pltpu.VMEM((2, tok, width), bf16),
            pltpu.VMEM((HALF * D, D), f32),
            pltpu.VMEM((HALF * D, D), bf16),
            pltpu.VMEM((HALF * D, D), bf16),
            pltpu.VMEM((CH, 3, D, D), bf16),
            pltpu.VMEM((CH, 3, D, D), bf16),
            pltpu.VMEM((CH, D, D), bf16),
            pltpu.VMEM((2, CH, NZ, SR, D), bf16),
            pltpu.VMEM((2, CH, SR, D), bf16),
            pltpu.VMEM((2, 2 * NY, CH, D, D), bf16),
            dma((CH, 2)),
            dma((4,)),
            pltpu.SemaphoreType.REGULAR((3,)),
            dma((7,)),
            dma((CH,)),
            dma((CH,)),
            dma((2, CH)),
            dma((2, 2, 3)),
            dma((2,)),
            dma((2, 2)),
            dma((2,)),
            dma((2, CH)),
        ],
        compiler_params=pltpu.CompilerParams(collective_id=0, has_side_effects=True),
    )(frame_len, window_back, level_weight, queries, keys, values)


def solution(mesh):
    return jax.shard_map(
        functools.partial(body, mesh.shape["space"]),
        mesh=mesh,
        in_specs=(
            P(("frame", "space"), None),
            P(("frame", "space"), None),
            P(("frame", "space"), None),
            P(None, None, ("frame", "space")),
            P(("frame", "space"), None),
            P(("frame", "space"), None),
        ),
        out_specs=P(("frame", "space"), None),
        check_vma=False,
    )
```
